32 devices in a mesh: row: 8 (over z, y), col: 4 (over x, core).
Axes of the slice: x: 2, y: 2, z: 4, core: 2. Of those that a mesh axis runs over, the one named last changes fastest.
Arguments:
- nodes_zero: float32 [8192, 64], P('row'), may hold values from -28 to 28
- nodes_one: float32 [8192, 64], P(('row', 'col')), may hold values from -28 to 28
- nodes_two: float32 [8192, 64], P('col'), may hold values from -28 to 28
- precision: float32 [64], replicated, may hold values from 0.1 to 0.4
- drift: float32 [64], replicated, may hold values from -1.2 to 1.2
- terminal: bfloat16 [8192, 128], P('col'), may hold values from -6 to 6
- exercise_one: float32 [8192, 128], P(('row', 'col')), may hold values from -6 to 6
- exercise_zero: float32 [8192, 128], P(('row', 'col')), may hold values from -6 to 6
- exercise_flags: int32 [2, 128], replicated, may hold values 0 or 1
Outputs:
- value_one: float32 [8192, 128], P(('row', 'col'))
- value_zero: float32 [8192, 128], P(('row', 'col'))
The draws below stay inside these ranges and needn't reach their ends.
All inputs are finite; a program needn't handle non-finite values.
Results may differ from the reference program's by a relative error of at most 0.0012.
Values may be sent and summed in bfloat16 or wider, within the bound.
A program may use at most 64 MiB of HBM per device.

```python
import math
import jax
import jax.numpy as jnp
from jax import lax

D = 64
TRADES = 128
SRC_DEV = 1024
NODES = 8192


def node_draw(key, date):
    own = jax.random.fold_in(key, 17 + date)
    drawn = jax.random.truncated_normal(own, -6.0, 6.0, (NODES, D), jnp.float32)
    if date == 0:
        return drawn
    direction = 1.0 if date == 2 else -1.0
    places = jax.random.randint(jax.random.fold_in(own, 5), (4,), 8, NODES).astype(jnp.int32)
    remote = direction * jax.random.uniform(jax.random.fold_in(own, 7), (4, D), jnp.float32, 26.0, 28.0)
    return drawn.at[places].set(remote)


def draw_nodes_zero(key, part):
    return node_draw(key, 0)


def draw_nodes_one(key, part):
    return node_draw(key, 1)


def draw_nodes_two(key, part):
    return node_draw(key, 2)


def set_ends(values, rng, least, high):
    longest = values.shape.index(max(values.shape))
    spots = []
    for shift in (0, 1):
        where = [jax.random.randint(jax.random.fold_in(rng, axis), (), 0, length) for axis, length in enumerate(values.shape)]
        where[longest] = (where[longest] + shift) % values.shape[longest]
        spots.append(tuple(where))
    return values.at[spots[0]].set(least).at[spots[1]].set(high)


def levels(own_key, shape, cuts, smallest, top_value):
    factor_of = 1.0
    for dim, parts in cuts:
        heights = jax.random.uniform(jax.random.fold_in(jax.random.fold_in(own_key, 6), dim), (parts,), jnp.float32, smallest / len(cuts), top_value / len(cuts))
        factor_of = factor_of * jnp.repeat(jnp.exp(heights), shape[dim] // parts).reshape((-1,) + (1,) * (len(shape) - 1 - dim))
    return factor_of


def scatter_about(rng, dims, deviation, most, cuts=(), kind=jnp.bfloat16):
    values = deviation * jax.random.normal(rng, dims, jnp.float32)
    if cuts:
        values = values * levels(rng, dims, cuts, -0.22, 0.18)
    return jnp.clip(values, -most, most).astype(kind)


def setup_inputs(seed: int = 0) -> dict:
    seeds = jax.random.split(jax.random.key(seed), 10)
    nodes_zero = draw_nodes_zero(jax.random.fold_in(seeds[9], 71), 0)
    nodes_one = draw_nodes_one(jax.random.fold_in(seeds[9], 71), 0)
    nodes_two = draw_nodes_two(jax.random.fold_in(seeds[9], 71), 0)
    precision = jnp.clip(jnp.exp(jax.random.uniform(seeds[3], (D,), jnp.float32, math.log(0.1), math.log(0.4))), 0.1, 0.4)
    drift = scatter_about(seeds[4], (D,), 0.3, 1.2, (), jnp.float32)
    terminal = scatter_about(seeds[5], (NODES, TRADES), 1.0, 6.0, ((0, 4),))
    exercise_one = scatter_about(seeds[6], (NODES, TRADES), 1.0, 6.0, ((0, 32),), jnp.float32)
    exercise_zero = scatter_about(seeds[7], (NODES, TRADES), 1.0, 6.0, ((0, 32),), jnp.float32)
    exercise_flags = set_ends((jax.random.randint(seeds[8], (2, TRADES), 0, 2) < 1).astype(jnp.int32), jax.random.fold_in(seeds[8], 1), 0, 1)
    return {"nodes_zero": nodes_zero, "nodes_one": nodes_one, "nodes_two": nodes_two, "precision": precision, "drift": drift, "terminal": terminal, "exercise_one": exercise_one, "exercise_zero": exercise_zero, "exercise_flags": exercise_flags}


def scores_of(queries, offsets, targets):
    product = lax.dot_general(queries, targets, (((1,), (1,)), ((), ())), preferred_element_type=jnp.float32)
    return product - offsets[:, None]


def continuation(sources, targets, prices, precision, drift):
    shifted = sources + drift
    queries = (shifted * precision).astype(jnp.bfloat16)
    offsets = 0.5 * jnp.sum(precision * shifted * shifted, axis=1)
    blocks = sources.shape[0] // SRC_DEV
    query_blocks = queries.reshape(blocks, SRC_DEV, -1)
    offset_blocks = offsets.reshape(blocks, SRC_DEV)

    def gather_stats(state, pieces):
        maxima, totals = state
        scores = scores_of(pieces[0], pieces[1], targets)
        highest = jnp.maximum(maxima, jnp.max(scores, axis=0))
        totals = totals * jnp.exp(maxima - highest) + jnp.sum(jnp.exp(scores - highest[None, :]), axis=0)
        return (highest, totals), None

    start_max = jnp.full((targets.shape[0],), -jnp.inf, jnp.float32)
    start_total = jnp.zeros((targets.shape[0],), jnp.float32)
    (maxima, totals), unused = lax.scan(gather_stats, (start_max, start_total), (query_blocks, offset_blocks))
    inverse = 1.0 / totals

    def carried(pieces):
        scores = scores_of(pieces[0], pieces[1], targets)
        weights = (jnp.exp(scores - maxima[None, :]) * inverse[None, :]).astype(jnp.bfloat16)
        return jnp.dot(weights, prices, preferred_element_type=jnp.float32)

    return lax.map(carried, (query_blocks, offset_blocks)).reshape(sources.shape[0], -1)


def settle(carried, exercise, allowed):
    return jnp.where(allowed[None, :] == 1, jnp.maximum(exercise, carried), carried)


def reference(nodes_zero, nodes_one, nodes_two, precision, drift, terminal, exercise_one, exercise_zero, exercise_flags):
    carry_one = continuation(nodes_one, nodes_two.astype(jnp.bfloat16), terminal, precision, drift)
    value_one = settle(carry_one, exercise_one, exercise_flags[1])
    carry_zero = continuation(nodes_zero, nodes_one.astype(jnp.bfloat16), value_one.astype(jnp.bfloat16), precision, drift)
    value_zero = settle(carry_zero, exercise_zero, exercise_flags[0])
    return value_one, value_zero
```

```python
import functools

import jax
import jax.numpy as jnp
from jax import lax
from jax.experimental import pallas as pl
from jax.experimental.pallas import tpu as pltpu
from jax.sharding import PartitionSpec as P

MESH = pl.DeviceIdType.MESH
TILE = 256
PARTS = 2
LIMIT = 60 * 1024 * 1024


def column_of(row):
    return jnp.broadcast_to(row, (128, row.shape[1])).T[:, :1]


def queries_of(nodes, precision, drift, height):
    shifted = nodes + drift
    offsets = 0.5 * jnp.sum(precision * shifted * shifted, axis=0, keepdims=True)
    first = offsets.astype(jnp.bfloat16).astype(jnp.float32)
    rest = offsets - first
    second = rest.astype(jnp.bfloat16).astype(jnp.float32)
    third = rest - second
    count = height - nodes.shape[0]
    at = lax.broadcasted_iota(jnp.int32, (count, nodes.shape[1]), 0)
    extra = jnp.where(at == 0, first, jnp.where(at == 1, second, jnp.where(at == 2, third, 0.0)))
    return jnp.concatenate([shifted * precision, extra], axis=0)


def upright(tall, lanes):
    short = lanes - tall.shape[0]
    if short:
        tall = jnp.concatenate([tall, jnp.zeros((short, tall.shape[1]), tall.dtype)], axis=0)
    return tall.T.astype(jnp.bfloat16)


def ones_under(count, width):
    at = lax.broadcasted_iota(jnp.int32, (count, width), 0)
    return jnp.where(at < 3, -1.0, 0.0).astype(jnp.bfloat16)


def body(
    rows,
    cols,
    nz_hbm,
    n1_hbm,
    n2_hbm,
    precision_hbm,
    drift_hbm,
    terminal_hbm,
    ex1_hbm,
    ex0_hbm,
    flags_hbm,
    v1_hbm,
    v0_hbm,
    precision_ref,
    drift_ref,
    flags_ref,
    nz_ref,
    n1_ref,
    n2_ref,
    terminal_ref,
    ex1_ref,
    ex0_ref,
    v1_ref,
    v0_ref,
    q1t,
    q1,
    t1,
    q0,
    t2,
    e1,
    e0,
    w0,
    st1,
    st0,
    f1,
    f0,
    price,
    out1,
    in1,
    out0,
    in0,
    q_send,
    q_recv,
    t_send,
    t_recv,
    s1_send,
    s1_recv,
    s0_send,
    s0_recv,
    p_send,
    p_recv,
    r1_send,
    r1_recv,
    r0_send,
    r0_recv,
    local,
):
    r = lax.axis_index("row")
    c = lax.axis_index("col")
    depth, own = n1_ref.shape
    sources = nz_ref.shape[1]
    lanes = q0.shape[1]
    height = q1t.shape[1]
    chunks, _, width = e1.shape
    barrier = pltpu.get_barrier_semaphore()
    for d in range(1, rows):
        pl.semaphore_signal(barrier, inc=1, device_id=(lax.rem(r + d, rows), c), device_id_type=MESH)
    for d in range(1, cols):
        pl.semaphore_signal(barrier, inc=1, device_id=(r, lax.rem(c + d, cols)), device_id_type=MESH)

    loads = [
        pltpu.make_async_copy(a, b, local.at[i])
        for i, (a, b) in enumerate(
            [
                (n1_hbm, n1_ref),
                (n2_hbm, n2_ref),
                (nz_hbm, nz_ref),
                (terminal_hbm, terminal_ref),
                (ex1_hbm, ex1_ref),
                (ex0_hbm, ex0_ref),
                (flags_hbm, flags_ref),
                (precision_hbm, precision_ref),
                (drift_hbm, drift_ref),
            ]
        )
    ]
    for load in loads[7:] + loads[:7]:
        load.start()
    loads[7].wait()
    loads[8].wait()
    precision = column_of(precision_ref[...])
    drift = column_of(drift_ref[...])
    loads[0].wait()
    mine = queries_of(n1_ref[...], precision, drift, height)
    q1t[c] = mine.astype(jnp.bfloat16)
    t1[r, :depth, :] = n1_ref[...].astype(jnp.bfloat16)
    for i in range(rows):
        t1[i, depth:, :] = ones_under(lanes - depth, own)
    loads[1].wait()
    for k in range(chunks):
        t2[k, :depth, :] = n2_ref[:, k * width : (k + 1) * width].astype(jnp.bfloat16)
        t2[k, depth:, :] = ones_under(lanes - depth, width)
    q1[c] = upright(mine, lanes)
    pl.semaphore_wait(barrier, rows + cols - 2)

    def to_rows(buf, send, recv):
        def make(d, slot):
            view = buf.at[slot, pl.ds(0, depth)] if buf is t1 else buf.at[slot]
            return pltpu.make_async_remote_copy(
                src_ref=view,
                dst_ref=view,
                send_sem=send.at[d],
                recv_sem=recv.at[d],
                device_id=(lax.rem(r + d, rows), c),
                device_id_type=MESH,
            )

        return make

    def start_rows(buf, send, recv):
        make = to_rows(buf, send, recv)
        for d in range(1, rows):
            make(d, r).start()

    def recv_rows(buf, send, recv):
        make = to_rows(buf, send, recv)
        for d in range(1, rows):
            make(d, lax.rem(r + rows - d, rows)).wait_recv()

    def sent_rows(buf, send, recv):
        make = to_rows(buf, send, recv)
        for d in range(1, rows):
            make(d, r).wait_send()

    def q_copy(d, slot):
        return pltpu.make_async_remote_copy(
            src_ref=q1t.at[slot],
            dst_ref=q1t.at[slot],
            send_sem=q_send.at[d],
            recv_sem=q_recv.at[d],
            device_id=(r, lax.rem(c + d, cols)),
            device_id_type=MESH,
        )

    for d in range(1, cols):
        q_copy(d, c).start()
    start_rows(t1, t_send, t_recv)

    loads[2].wait()
    q0[...] = upright(queries_of(nz_ref[...], precision, drift, height), lanes)
    step = min(TILE, sources)

    def stats(load_queries, load_targets, e, st, begin, end):
        def one(k, carry):
            target = load_targets(k)
            peak = None
            for at in range(0, sources, step):
                s = lax.dot_general(
                    load_queries(at), target, (((1,), (0,)), ((), ())), preferred_element_type=jnp.float32
                )
                e[k, at : at + step, :] = s
                top = jnp.max(s.reshape(step // 8, 8, width), axis=0)
                peak = top if peak is None else jnp.maximum(peak, top)
            peak = jnp.max(peak, axis=0, keepdims=True)
            total = jnp.zeros((8, width), jnp.float32)
            for at in range(0, sources, step):
                x = jnp.exp(e[k, at : at + step, :] - peak)
                e[k, at : at + step, :] = x
                total = total + jnp.sum(x.reshape(step // 8, 8, width), axis=0)
            st[r, 0, pl.ds(k, 1), :] = peak
            st[r, 1, pl.ds(k, 1), :] = jnp.sum(total, axis=0, keepdims=True)
            return carry

        lax.fori_loop(begin, end, one, 0)

    def factor(st, f):
        peak = st[0, 0]
        for i in range(1, rows):
            peak = jnp.maximum(peak, st[i, 0])
        total = jnp.zeros_like(peak)
        for i in range(rows):
            total = total + st[i, 1] * jnp.exp(st[i, 0] - peak)
        f[...] = jnp.exp(st[r, 0] - peak) * (1.0 / total)

    for d in range(1, cols):
        slot = lax.rem(c + cols - d, cols)
        q_copy(d, slot).wait_recv()
        q1[slot] = upright(q1t[slot].astype(jnp.float32), lanes)

    def q1_rows(at):
        return q1[at // own : (at + step) // own].reshape(step, q1.shape[2])

    stats(q1_rows, lambda k: t2[k], e1, st1, 0, chunks)
    start_rows(st1, s1_send, s1_recv)

    recv_rows(t1, t_send, t_recv)
    per = width // own

    def t1_rows(k):
        if per == 1:
            return t1[k]
        return jnp.concatenate([t1[k * per + i] for i in range(per)], axis=1)

    def stats_zero(begin, end):
        stats(lambda at: q0[at : at + step, :], t1_rows, e0, st0, begin, end)

    half = (chunks + 1) // 2
    stats_zero(0, half)

    recv_rows(st1, s1_send, s1_recv)
    factor(st1, f1)

    def partial_of(weights, load_prices, first, count):
        total = jnp.zeros((count, v1_ref.shape[1]), jnp.float32)
        for k in range(chunks):
            total = total + jnp.dot(weights(k, first, count), load_prices(k), preferred_element_type=jnp.float32)
        return total

    def carry_copy(out, into, send, recv, d, h, count):
        return pltpu.make_async_remote_copy(
            src_ref=out.at[d, pl.ds(h * count, count)],
            dst_ref=into.at[d, pl.ds(h * count, count)],
            send_sem=send.at[h * cols + d],
            recv_sem=recv.at[h * cols + d],
            device_id=(r, lax.rem(c + d, cols)),
            device_id_type=MESH,
        )

    def send_carry(weights, load_prices, out, into, send, recv, parts):
        count = own // parts
        for h in range(parts):
            for d in range(1, cols):
                first = lax.rem(c + d, cols) * own + h * count
                part = partial_of(weights, load_prices, first, count)
                out[d, h * count : (h + 1) * count, :] = part.astype(out.dtype)
                carry_copy(out, into, send, recv, d, h, count).start()
        return partial_of(weights, load_prices, c * own, own)

    def take_carry(total, out, into, send, recv, parts, h):
        count = own // parts
        piece = slice(h * count, (h + 1) * count)
        total = total[piece]
        for d in range(1, cols):
            carry_copy(out, into, send, recv, d, h, count).wait_recv()
            total = total + into[d, piece, :].astype(jnp.float32)
        return total

    def end_carry(out, into, send, recv, parts):
        for h in range(parts):
            for d in range(1, cols):
                carry_copy(out, into, send, recv, d, h, own // parts).wait_send()

    def weights_one(k, first, count):
        return (e1[k, pl.ds(first, count), :] * f1[pl.ds(k, 1), :]).astype(jnp.bfloat16)

    loads[3].wait()
    one = (out1, in1, r1_send, r1_recv, PARTS)
    held = send_carry(weights_one, lambda k: terminal_ref[k * width : (k + 1) * width, :], *one)
    stats_zero(half, chunks)
    start_rows(st0, s0_send, s0_recv)
    loads[4].wait()
    loads[6].wait()
    partner = r + 1 - 2 * lax.rem(r, 2)
    half_rows = rows // 2

    size = own // PARTS

    def along(k, h, slot):
        view = price.at[slot, pl.ds(h * size, size)]
        return pltpu.make_async_remote_copy(
            src_ref=view,
            dst_ref=view,
            send_sem=p_send.at[h * rows + k],
            recv_sem=p_recv.at[h * rows + k],
            device_id=(lax.rem(r + 2 * k, rows), c),
            device_id_type=MESH,
        )

    def across(k, h, slot):
        view = price.at[slot, pl.ds(h * size, size)]
        return pltpu.make_async_remote_copy(
            src_ref=view,
            dst_ref=view,
            send_sem=p_send.at[h * rows + half_rows + k],
            recv_sem=p_recv.at[h * rows + half_rows + k],
            device_id=(partner, c),
            device_id_type=MESH,
        )

    for h in range(PARTS):
        piece = slice(h * size, (h + 1) * size)
        carried = take_carry(held, *one, h)
        value = jnp.where(flags_ref[1:2, :] == 1, jnp.maximum(ex1_ref[piece, :], carried), carried)
        v1_ref[piece, :] = value
        price[r, piece, :] = value.astype(jnp.bfloat16)
        for k in range(1, half_rows):
            along(k, h, r).start()
        across(0, h, r).start()
    v1_hbm[...] = v1_ref[...]

    recv_rows(st0, s0_send, s0_recv)
    factor(st0, f0)

    def weigh(k, carry):
        for at in range(0, sources, step):
            w0[k, at : at + step, :] = (e0[k, at : at + step, :] * f0[pl.ds(k, 1), :]).astype(jnp.bfloat16)
        return carry

    lax.fori_loop(0, chunks, weigh, 0)
    for h in range(PARTS):
        for k in range(1, half_rows):
            slot = lax.rem(r + rows - 2 * k, rows)
            along(k, h, slot).wait_recv()
            across(k, h, slot).start()
    for h in range(PARTS):
        for k in range(half_rows):
            across(k, h, lax.rem(partner + rows - 2 * k, rows)).wait_recv()

    def price_rows(k):
        return price[k * per : (k + 1) * per].reshape(width, price.shape[2])

    def weights_zero(k, first, count):
        return w0[k, pl.ds(first, count), :]

    zero = (out0, in0, r0_send, r0_recv, 1)
    held = send_carry(weights_zero, price_rows, *zero)
    loads[5].wait()
    carried = take_carry(held, *zero, 0)
    v0_ref[...] = jnp.where(flags_ref[0:1, :] == 1, jnp.maximum(ex0_ref[...], carried), carried)
    v0_hbm[...] = v0_ref[...]

    for d in range(1, cols):
        q_copy(d, c).wait_send()
    sent_rows(t1, t_send, t_recv)
    sent_rows(st1, s1_send, s1_recv)
    sent_rows(st0, s0_send, s0_recv)
    for h in range(PARTS):
        for k in range(half_rows):
            across(k, h, r).wait_send()
            if k:
                along(k, h, r).wait_send()
    end_carry(*one)
    end_carry(*zero)


def shards(rows, cols, nodes_zero, nodes_one, nodes_two, precision, drift, terminal, ex1, ex0, flags):
    own, depth = nodes_one.shape
    height = depth + 16
    sources = nodes_zero.shape[0]
    targets = nodes_two.shape[0]
    trades = terminal.shape[1]
    width = max(own, min(TILE, targets))
    chunks = targets // width
    lanes = 128 * (-(-(depth + 3) // 128))
    dma = pltpu.SemaphoreType.DMA
    out = jax.ShapeDtypeStruct((own, trades), jnp.float32)
    stat = pltpu.VMEM((rows, 2, chunks, width), jnp.float32)
    tall = pltpu.VMEM((chunks, sources, width), jnp.float32)
    few = pltpu.VMEM((chunks, width), jnp.float32)
    parts = pltpu.VMEM((cols, own, trades), jnp.float32)
    slim = pltpu.VMEM((cols, own, trades), jnp.bfloat16)
    anywhere = pl.BlockSpec(memory_space=pltpu.VMEM)
    mine = pltpu.VMEM((own, trades), jnp.float32)
    one, zero = pl.pallas_call(
        functools.partial(body, rows, cols),
        out_shape=(pltpu.VMEM((own, trades), jnp.float32),) * 2,
        in_specs=[pl.BlockSpec(memory_space=pltpu.HBM)] * 9,
        out_specs=(anywhere, anywhere),
        scratch_shapes=[
            pltpu.VMEM((1, depth), jnp.float32),
            pltpu.VMEM((1, depth), jnp.float32),
            pltpu.VMEM((2, trades), jnp.int32),
            pltpu.VMEM((depth, sources), jnp.float32),
            pltpu.VMEM((depth, own), jnp.float32),
            pltpu.VMEM((depth, targets), jnp.float32),
            pltpu.VMEM((targets, trades), jnp.bfloat16),
            mine,
            mine,
            mine,
            mine,
            pltpu.VMEM((cols, height, own), jnp.bfloat16),
            pltpu.VMEM((cols, own, lanes), jnp.bfloat16),
            pltpu.VMEM((rows, lanes, own), jnp.bfloat16),
            pltpu.VMEM((sources, lanes), jnp.bfloat16),
            pltpu.VMEM((chunks, lanes, width), jnp.bfloat16),
            tall,
            tall,
            pltpu.VMEM((chunks, sources, width), jnp.bfloat16),
            stat,
            stat,
            few,
            few,
            pltpu.VMEM((rows, own, trades), jnp.bfloat16),
            parts,
            parts,
            slim,
            slim,
            *[dma((cols,))] * 2,
            *[dma((rows,))] * 6,
            *[dma((PARTS * rows,))] * 2,
            *[dma((PARTS * cols,))] * 2,
            *[dma((cols,))] * 2,
            dma((11,)),
        ],
        compiler_params=pltpu.CompilerParams(
            collective_id=0, has_side_effects=True, vmem_limit_bytes=LIMIT
        ),
    )(nodes_zero.T, nodes_one.T, nodes_two.T, precision[None, :], drift[None, :], terminal, ex1, ex0, flags)
    return handed(one, zero)


def hand(a, b, c, d, sems):
    copies = [pltpu.make_async_copy(a, c, sems.at[0]), pltpu.make_async_copy(b, d, sems.at[1])]
    for copy in copies:
        copy.start()
    for copy in copies:
        copy.wait()


def handed(one, zero):
    here = pl.BlockSpec(memory_space=pltpu.VMEM)
    out = jax.ShapeDtypeStruct(one.shape, one.dtype)
    return pl.pallas_call(
        hand,
        out_shape=(out, out),
        in_specs=[here, here],
        out_specs=(pl.BlockSpec(memory_space=pltpu.HBM),) * 2,
        scratch_shapes=[pltpu.SemaphoreType.DMA((2,))],
        compiler_params=pltpu.CompilerParams(vmem_limit_bytes=2 * 1024 * 1024),
    )(one, zero)


def solution(mesh):
    both = P(("row", "col"), None)
    return jax.shard_map(
        functools.partial(shards, mesh.shape["row"], mesh.shape["col"]),
        mesh=mesh,
        in_specs=(P("row", None), both, P("col", None), P(), P(), P("col", None), both, both, P()),
        out_specs=(both, both),
        check_vma=False,
    )
```

```python
import functools

import jax
import jax.numpy as jnp
from jax import lax
from jax.experimental import pallas as pl
from jax.experimental.pallas import tpu as pltpu
from jax.sharding import PartitionSpec as P

MESH = pl.DeviceIdType.MESH
TILE = 256
PARTS = 2
LAST = 2
LIMIT = 60 * 1024 * 1024


def flip(index, mask, size):
    bit = 1
    while bit < size:
        if mask & bit:
            index = index + bit - 2 * bit * lax.rem(lax.div(index, bit), 2)
        bit *= 2
    return index


def column_of(row):
    return jnp.broadcast_to(row, (128, row.shape[1])).T[:, :1]


def queries_of(nodes, precision, drift, height):
    shifted = nodes + drift
    offsets = 0.5 * jnp.sum(precision * shifted * shifted, axis=0, keepdims=True)
    first = offsets.astype(jnp.bfloat16).astype(jnp.float32)
    rest = offsets - first
    second = rest.astype(jnp.bfloat16).astype(jnp.float32)
    third = rest - second
    count = height - nodes.shape[0]
    at = lax.broadcasted_iota(jnp.int32, (count, nodes.shape[1]), 0)
    extra = jnp.where(at == 0, first, jnp.where(at == 1, second, jnp.where(at == 2, third, 0.0)))
    return jnp.concatenate([shifted * precision, extra], axis=0)


def upright(tall, lanes):
    short = lanes - tall.shape[0]
    if short:
        tall = jnp.concatenate([tall, jnp.zeros((short, tall.shape[1]), tall.dtype)], axis=0)
    return tall.T.astype(jnp.bfloat16)


def ones_under(count, width):
    at = lax.broadcasted_iota(jnp.int32, (count, width), 0)
    return jnp.where(at < 3, -1.0, 0.0).astype(jnp.bfloat16)


def settled(allowed, exercise, carried):
    return jnp.where(allowed == 1, jnp.maximum(exercise, carried), carried)


def scored(queries, targets):
    s = lax.dot_general(queries, targets, (((1,), (0,)), ((), ())), preferred_element_type=jnp.float32)
    fold = (s.shape[0] // 8, 8, s.shape[1])
    peak = jnp.max(jnp.max(s.reshape(fold), axis=0), axis=0, keepdims=True)
    x = jnp.exp(s - peak)
    return x, peak, jnp.sum(jnp.sum(x.reshape(fold), axis=0), axis=0, keepdims=True)


def merged(levels, totals):
    top = functools.reduce(jnp.maximum, levels)
    total = None
    for i, level in enumerate(levels):
        term = jnp.exp(level - top)
        if totals is not None:
            term = totals[i] * term
        total = term if total is None else total + term
    return top + jnp.log(total)


def body(
    rows,
    cols,
    nz_hbm,
    n1_hbm,
    n2_hbm,
    precision_hbm,
    drift_hbm,
    terminal_hbm,
    ex1_hbm,
    ex0_hbm,
    flags_hbm,
    v1_ref,
    v0_ref,
    precision_ref,
    drift_ref,
    flags_ref,
    nz_ref,
    n1_ref,
    n2_ref,
    terminal_ref,
    ex1_ref,
    ex0_ref,
    q1t,
    q1,
    t1,
    q0a,
    q0,
    t2,
    e1,
    e0,
    pk1,
    tt1,
    f1,
    pk0,
    tt0,
    f0,
    l1,
    l0,
    price,
    acc1,
    acc0,
    pair_out1,
    pair_in1,
    far_out1,
    far_in1,
    pair_out0,
    pair_in0,
    far_out0,
    far_in0,
    q_send,
    q_recv,
    t_send,
    t_recv,
    l1_send,
    l1_recv,
    l0_send,
    l0_recv,
    p_send,
    p_recv,
    pair1_send,
    pair1_recv,
    far1_send,
    far1_recv,
    pair0_send,
    pair0_recv,
    far0_send,
    far0_recv,
    local,
):
    r = lax.axis_index("row")
    c = lax.axis_index("col")
    depth, own = n1_ref.shape
    lanes = q0.shape[1]
    height = q1t.shape[1]
    _, chunks, _, width = e1.shape
    trades = price.shape[2]
    sources = q0.shape[0]
    blocks, _, _ = pk0.shape
    step = sources // blocks
    halves = l1.shape[1]
    some = chunks // halves

    def row_peer(m):
        return (flip(r, m, rows), c)

    def col_peer(s):
        return (r, flip(c, s, cols))

    def remote(src, dst, send, recv, peer):
        return pltpu.make_async_remote_copy(
            src_ref=src, dst_ref=dst, send_sem=send, recv_sem=recv, device_id=peer, device_id_type=MESH
        )

    barrier = pltpu.get_barrier_semaphore()
    for m in range(1, rows):
        pl.semaphore_signal(barrier, inc=1, device_id=row_peer(m), device_id_type=MESH)
    for s in range(1, cols):
        pl.semaphore_signal(barrier, inc=1, device_id=col_peer(s), device_id_type=MESH)
    loads = [
        pltpu.make_async_copy(a, b, local.at[i])
        for i, (a, b) in enumerate(
            [
                (precision_hbm, precision_ref),
                (drift_hbm, drift_ref),
                (n1_hbm, n1_ref),
                (n2_hbm, n2_ref),
                (nz_hbm, nz_ref),
                (terminal_hbm, terminal_ref),
                (ex1_hbm, ex1_ref),
                (flags_hbm, flags_ref),
                (ex0_hbm, ex0_ref),
            ]
        )
    ]
    for load in loads:
        load.start()
    for load in loads[:3]:
        load.wait()
    precision = column_of(precision_ref[...])
    drift = column_of(drift_ref[...])
    mine = queries_of(n1_ref[...], precision, drift, height)
    q1t[0] = mine.astype(jnp.bfloat16)
    t1[0, :depth, :] = n1_ref[...].astype(jnp.bfloat16)
    pl.semaphore_wait(barrier, rows + cols - 2)

    def q_copy(s):
        return remote(q1t.at[0], q1t.at[s], q_send.at[s], q_recv.at[s], col_peer(s))

    far_first = list(range(2, cols, 2)) + list(range(3, cols, 2)) + [1]
    for s in far_first:
        q_copy(s).start()

    def t_copy(m):
        if m % 2:
            src, peer = t1.at[m - 1, pl.ds(0, depth)], row_peer(1)
        else:
            src, peer = t1.at[0, pl.ds(0, depth)], row_peer(m)
        return remote(src, t1.at[m, pl.ds(0, depth)], t_send.at[m], t_recv.at[m], peer)

    for m in range(2, rows, 2):
        t_copy(m).start()
    t_copy(1).start()

    q1[0] = upright(mine, lanes)
    for m in range(rows):
        t1[m, depth:, :] = ones_under(lanes - depth, own)
    loads[3].wait()
    for k in range(chunks):
        t2[k, :depth, :] = n2_ref[:, k * width : (k + 1) * width].astype(jnp.bfloat16)
        t2[k, depth:, :] = ones_under(lanes - depth, width)

    def stats_one(s, first, last):
        for k in range(first, last):
            x, peak, total = scored(q1[s], t2[k])
            e1[s, k] = x
            pk1[s, k : k + 1, :] = peak
            tt1[s, k : k + 1, :] = total

    def stats_zero(m):
        row = flip(r, m, rows)
        for b in range(blocks):
            x, peak, total = scored(q0[b * step : (b + 1) * step, :], t1[m])
            e0[m, b * step : (b + 1) * step, :] = x
            pk0[b, pl.ds(row, 1), :] = peak
            tt0[b, pl.ds(row, 1), :] = total

    def take_q(s):
        q_copy(s).wait_recv()
        q1[s] = upright(q1t[s].astype(jnp.float32), lanes)

    stats_one(0, 0, chunks)
    take_q(1)
    stats_one(1, 0, chunks)
    loads[4].wait()
    q0a[...] = upright(queries_of(nz_ref[...], precision, drift, height), lanes)
    for s in range(cols):
        q0[s * own : (s + 1) * own, :] = q0a[pl.ds(pl.multiple_of(flip(c, s, cols) * own, own), own), :]
    stats_zero(0)
    for s in far_first[:-2]:
        take_q(s)
        stats_one(s, 0, chunks)

    def l1_copy(m, h):
        at = h * rows + m
        return remote(l1.at[0, h], l1.at[m, h], l1_send.at[at], l1_recv.at[at], row_peer(m))

    final = far_first[-2] if cols > 2 else None
    if final is not None:
        take_q(final)
    for h in range(halves):
        part = slice(h * some, (h + 1) * some)
        if final is not None:
            stats_one(final, h * some, (h + 1) * some)
        l1[0, h] = merged([pk1[s, part, :] for s in range(cols)], [tt1[s, part, :] for s in range(cols)])
        for m in range(1, rows):
            l1_copy(m, h).start()

    for m in range(2, rows, 2):
        t_copy(m).wait_recv()
        t_copy(m + 1).start()
    for m in range(2, rows, 2):
        stats_zero(m)
    t_copy(1).wait_recv()
    stats_zero(1)

    def weights_one(s, k):
        return (e1[s, k] * f1[s, k : k + 1, :]).astype(jnp.bfloat16)

    def partial_one(s, total, first, last):
        for k in range(first, last):
            part = jnp.dot(
                weights_one(s, k), terminal_ref[k * width : (k + 1) * width, :], preferred_element_type=jnp.float32
            )
            total = part if total is None else total + part
        return total

    def pair_copy(out, into, send, recv, s):
        return remote(out.at[s // 2], into.at[s // 2], send.at[s // 2], recv.at[s // 2], col_peer(1))

    def far_copy(out, into, send, recv, s, h, count):
        at = h * (cols // 2) + s // 2
        piece = pl.ds(h * count, count)
        return remote(out.at[s // 2, piece], into.at[s // 2, piece], send.at[at], recv.at[at], col_peer(s))

    pair1 = (pair_out1, pair_in1, pair1_send, pair1_recv)
    far1 = (far_out1, far_in1, far1_send, far1_recv)
    pair0 = (pair_out0, pair_in0, pair0_send, pair0_recv)
    far0 = (far_out0, far_in0, far0_send, far0_recv)
    size = own // PARTS
    away = list(range(2, cols, 2))

    for h in range(halves):
        part = slice(h * some, (h + 1) * some)
        for m in range(1, rows):
            l1_copy(m, h).wait_recv()
        if h == 0:
            loads[5].wait()
        level = merged([l1[m, h] for m in range(rows)], None)
        for s in range(cols):
            f1[s, part, :] = jnp.exp(pk1[s, part, :] - level)
        last = h == halves - 1
        for s in [s + 1 for s in away] + [1] + away + [0]:
            total = partial_one(s, acc1[s] if h else None, h * some, (h + 1) * some)
            if last and s % 2:
                pair_out1[s // 2] = total
                pair_copy(*pair1, s - 1).start()
            else:
                acc1[s] = total
    for s in away:
        pair_copy(*pair1, s).wait_recv()
        for h in range(PARTS):
            piece = slice(h * size, (h + 1) * size)
            far_out1[s // 2, piece, :] = acc1[s, piece, :] + pair_in1[s // 2, piece, :]
            far_copy(*far1, s, h, size).start()
    pair_copy(*pair1, 0).wait_recv()
    held = acc1[0] + pair_in1[0]

    for m in range(3, rows, 2):
        t_copy(m).wait_recv()
        stats_zero(m)
    l0[0] = merged([pk0[b] for b in range(blocks)], [tt0[b] for b in range(blocks)])

    def l0_copy(m):
        return remote(l0.at[0], l0.at[m], l0_send.at[m], l0_recv.at[m], row_peer(m))

    for m in range(1, rows):
        l0_copy(m).start()
    loads[6].wait()
    loads[7].wait()

    def p_copy(m, h):
        piece = pl.ds(h * size, size)
        at = h * rows + m
        if m % 2:
            src, peer = price.at[m - 1, piece], row_peer(1)
        else:
            src, peer = price.at[0, piece], row_peer(m)
        return remote(src, price.at[m, piece], p_send.at[at], p_recv.at[at], peer)

    for h in range(PARTS):
        piece = slice(h * size, (h + 1) * size)
        carried = held[piece]
        for s in away:
            far_copy(*far1, s, h, size).wait_recv()
            carried = carried + far_in1[s // 2, piece, :]
        value = settled(flags_ref[1:2, :], ex1_ref[piece, :], carried)
        price[0, piece, :] = value.astype(jnp.bfloat16)
        v1_ref[piece, :] = value
        for m in range(2, rows, 2):
            p_copy(m, h).start()
        p_copy(1, h).start()

    for m in range(1, rows):
        l0_copy(m).wait_recv()
    level = merged([l0[m] for m in range(rows)], None)
    for b in range(blocks):
        f0[b] = jnp.exp(pk0[b] - level)

    def add_zero(m, first, count):
        row = flip(r, m, rows)
        parts = []
        each = min(step, count)
        for at in range(first, first + count, each):
            w = (e0[m, at : at + each, :] * f0[at // step, pl.ds(row, 1), :]).astype(jnp.bfloat16)
            parts.append(jnp.dot(w, price[m], preferred_element_type=jnp.float32))
        return parts[0] if len(parts) == 1 else jnp.concatenate(parts, axis=0)

    def gain(m):
        for at in range(0, sources, step):
            part = add_zero(m, at, step)
            acc0[at : at + step, :] = part if m == 0 else acc0[at : at + step, :] + part

    gain(0)
    for h in range(PARTS):
        for m in range(2, rows, 2):
            p_copy(m, h).wait_recv()
            p_copy(m + 1, h).start()
    for m in range(2, rows, 2):
        gain(m)
    for m in range(1, rows - 2, 2):
        for h in range(PARTS):
            p_copy(m, h).wait_recv()
        gain(m)
    for h in range(PARTS):
        p_copy(rows - 1, h).wait_recv()
    count = own // LAST
    for s in [s + 1 for s in away] + [1] + away + [0]:
        total = acc0[s * own : (s + 1) * own, :] + add_zero(rows - 1, s * own, own)
        if s % 2:
            pair_out0[s // 2] = total
            pair_copy(*pair0, s - 1).start()
        else:
            acc0[s * own : (s + 1) * own, :] = total
    for s in away:
        pair_copy(*pair0, s).wait_recv()
        for h in range(LAST):
            piece = slice(h * count, (h + 1) * count)
            total = acc0[s * own + h * count : s * own + (h + 1) * count, :] + pair_in0[s // 2, piece, :]
            far_out0[s // 2, piece, :] = total.astype(far_out0.dtype)
            far_copy(*far0, s, h, count).start()
    pair_copy(*pair0, 0).wait_recv()
    held = acc0[:own, :] + pair_in0[0]
    loads[8].wait()
    for h in range(LAST):
        piece = slice(h * count, (h + 1) * count)
        carried = held[piece]
        for s in away:
            far_copy(*far0, s, h, count).wait_recv()
            carried = carried + far_in0[s // 2, piece, :].astype(jnp.float32)
        v0_ref[piece, :] = settled(flags_ref[0:1, :], ex0_ref[piece, :], carried)

    for s in range(1, cols):
        q_copy(s).wait_send()
    for m in range(1, rows):
        t_copy(m).wait_send()
        l0_copy(m).wait_send()
        for h in range(halves):
            l1_copy(m, h).wait_send()
        for h in range(PARTS):
            p_copy(m, h).wait_send()
    for s in range(0, cols, 2):
        pair_copy(*pair1, s).wait_send()
        pair_copy(*pair0, s).wait_send()
    for s in away:
        for h in range(PARTS):
            far_copy(*far1, s, h, size).wait_send()
        for h in range(LAST):
            far_copy(*far0, s, h, count).wait_send()


def shards(rows, cols, nodes_zero, nodes_one, nodes_two, precision, drift, terminal, ex1, ex0, flags):
    own, depth = nodes_one.shape
    height = depth + 16
    sources = nodes_zero.shape[0]
    targets = nodes_two.shape[0]
    trades = terminal.shape[1]
    width = min(TILE, targets)
    chunks = targets // width
    halves = 2 if chunks % 2 == 0 else 1
    step = max(own, min(TILE, sources))
    blocks = sources // step
    lanes = 128 * (-(-(depth + 3) // 128))
    dma = pltpu.SemaphoreType.DMA
    f32, bf16 = jnp.float32, jnp.bfloat16
    row_stat = pltpu.VMEM((cols, chunks, width), f32)
    col_stat = pltpu.VMEM((blocks, rows, own), f32)
    piece = pltpu.VMEM((cols // 2, own, trades), f32)
    slim = pltpu.VMEM((cols // 2, own, trades), bf16)
    mine = pltpu.VMEM((own, trades), f32)
    one, zero = pl.pallas_call(
        functools.partial(body, rows, cols),
        out_shape=(pltpu.VMEM((own, trades), f32),) * 2,
        in_specs=[pl.BlockSpec(memory_space=pltpu.HBM)] * 9,
        out_specs=(pl.BlockSpec(memory_space=pltpu.VMEM),) * 2,
        scratch_shapes=[
            pltpu.VMEM((1, depth), f32),
            pltpu.VMEM((1, depth), f32),
            pltpu.VMEM((2, trades), jnp.int32),
            pltpu.VMEM((depth, sources), f32),
            pltpu.VMEM((depth, own), f32),
            pltpu.VMEM((depth, targets), f32),
            pltpu.VMEM((targets, trades), bf16),
            mine,
            mine,
            pltpu.VMEM((cols, height, own), bf16),
            pltpu.VMEM((cols, own, lanes), bf16),
            pltpu.VMEM((rows, lanes, own), bf16),
            pltpu.VMEM((sources, lanes), bf16),
            pltpu.VMEM((sources, lanes), bf16),
            pltpu.VMEM((chunks, lanes, width), bf16),
            pltpu.VMEM((cols, chunks, own, width), f32),
            pltpu.VMEM((rows, sources, own), f32),
            row_stat,
            row_stat,
            row_stat,
            col_stat,
            col_stat,
            col_stat,
            pltpu.VMEM((rows, halves, chunks // halves, width), f32),
            pltpu.VMEM((rows, rows, own), f32),
            pltpu.VMEM((rows, own, trades), bf16),
            pltpu.VMEM((cols, own, trades), f32),
            pltpu.VMEM((sources, trades), f32),
            *[piece] * 6,
            *[slim] * 2,
            *[dma((cols,))] * 2,
            *[dma((rows,))] * 2,
            *[dma((halves * rows,))] * 2,
            *[dma((rows,))] * 2,
            *[dma((PARTS * rows,))] * 2,
            *[dma((cols // 2,))] * 2,
            *[dma((PARTS * (cols // 2),))] * 2,
            *[dma((cols // 2,))] * 2,
            *[dma((LAST * (cols // 2),))] * 2,
            dma((9,)),
        ],
        compiler_params=pltpu.CompilerParams(
            collective_id=0, has_side_effects=True, vmem_limit_bytes=LIMIT
        ),
    )(nodes_zero.T, nodes_one.T, nodes_two.T, precision[None, :], drift[None, :], terminal, ex1, ex0, flags)
    return handed(one, zero)


def hand(a, b, c, d, sems):
    copies = [pltpu.make_async_copy(a, c, sems.at[0]), pltpu.make_async_copy(b, d, sems.at[1])]
    for copy in copies:
        copy.start()
    for copy in copies:
        copy.wait()


def handed(one, zero):
    here = pl.BlockSpec(memory_space=pltpu.VMEM)
    out = jax.ShapeDtypeStruct(one.shape, one.dtype)
    return pl.pallas_call(
        hand,
        out_shape=(out, out),
        in_specs=[here, here],
        out_specs=(pl.BlockSpec(memory_space=pltpu.HBM),) * 2,
        scratch_shapes=[pltpu.SemaphoreType.DMA((2,))],
        compiler_params=pltpu.CompilerParams(vmem_limit_bytes=2 * 1024 * 1024),
    )(one, zero)


def solution(mesh):
    both = P(("row", "col"), None)
    return jax.shard_map(
        functools.partial(shards, mesh.shape["row"], mesh.shape["col"]),
        mesh=mesh,
        in_specs=(P("row", None), both, P("col", None), P(), P(), P("col", None), both, both, P()),
        out_specs=(both, both),
        check_vma=False,
    )
```

```python
import functools

import jax
import jax.numpy as jnp
from jax import lax
from jax.experimental import pallas as pl
from jax.experimental.pallas import tpu as pltpu
from jax.sharding import PartitionSpec as P

MESH = pl.DeviceIdType.MESH
TILE = 256
PARTS = 2
RELAY = 1
LAST = 2
LIMIT = 60 * 1024 * 1024


def flip(index, mask, size):
    bit = 1
    while bit < size:
        if mask & bit:
            index = index + bit - 2 * bit * lax.rem(lax.div(index, bit), 2)
        bit *= 2
    return index


def column_of(row):
    return jnp.broadcast_to(row, (128, row.shape[1])).T[:, :1]


def queries_of(nodes, precision, drift, height):
    shifted = nodes + drift
    offsets = 0.5 * jnp.sum(precision * shifted * shifted, axis=0, keepdims=True)
    first = offsets.astype(jnp.bfloat16).astype(jnp.float32)
    rest = offsets - first
    second = rest.astype(jnp.bfloat16).astype(jnp.float32)
    third = rest - second
    count = height - nodes.shape[0]
    at = lax.broadcasted_iota(jnp.int32, (count, nodes.shape[1]), 0)
    extra = jnp.where(at == 0, first, jnp.where(at == 1, second, jnp.where(at == 2, third, 0.0)))
    return jnp.concatenate([shifted * precision, extra], axis=0)


def upright(tall, lanes):
    short = lanes - tall.shape[0]
    if short:
        tall = jnp.concatenate([tall, jnp.zeros((short, tall.shape[1]), tall.dtype)], axis=0)
    return tall.T.astype(jnp.bfloat16)


def ones_under(count, width):
    at = lax.broadcasted_iota(jnp.int32, (count, width), 0)
    return jnp.where(at < 3, -1.0, 0.0).astype(jnp.bfloat16)


def settled(allowed, exercise, carried):
    return jnp.where(allowed == 1, jnp.maximum(exercise, carried), carried)


def scored(queries, targets):
    s = lax.dot_general(queries, targets, (((1,), (0,)), ((), ())), preferred_element_type=jnp.float32)
    fold = (s.shape[0] // 8, 8, s.shape[1])
    peak = jnp.max(jnp.max(s.reshape(fold), axis=0), axis=0, keepdims=True)
    x = jnp.exp(s - peak)
    return x, peak, jnp.sum(jnp.sum(x.reshape(fold), axis=0), axis=0, keepdims=True)


def merged(levels, totals):
    top = functools.reduce(jnp.maximum, levels)
    total = None
    for i, level in enumerate(levels):
        term = jnp.exp(level - top)
        if totals is not None:
            term = totals[i] * term
        total = term if total is None else total + term
    return top + jnp.log(total)


def body(
    rows,
    cols,
    nz_hbm,
    n1_hbm,
    n2_hbm,
    precision_hbm,
    drift_hbm,
    terminal_hbm,
    ex1_hbm,
    ex0_hbm,
    flags_hbm,
    v1_out,
    v0_out,
    precision_ref,
    drift_ref,
    flags_ref,
    nz_ref,
    n1_ref,
    n2_ref,
    terminal_ref,
    ex1_ref,
    ex0_ref,
    v1_ref,
    v0_ref,
    q1t,
    q1,
    t1,
    q0a,
    q0,
    t2,
    e1,
    e0,
    pk1,
    tt1,
    f1,
    pk0,
    tt0,
    f0,
    l1,
    l0,
    price,
    acc1,
    acc0,
    pair_out1,
    pair_in1,
    far_out1,
    far_in1,
    far_out0,
    far_in0,
    q_send,
    q_recv,
    t_send,
    t_recv,
    l1_send,
    l1_recv,
    l0_send,
    l0_recv,
    p_send,
    p_recv,
    pc_recv,
    pair1_send,
    pair1_recv,
    far1_send,
    far1_recv,
    y_send,
    y_recv,
    far0_send,
    far0_recv,
    local,
    ready,
):
    r = lax.axis_index("row")
    c = lax.axis_index("col")
    depth, own = n1_ref.shape
    lanes = q0.shape[1]
    height = q1t.shape[1]
    _, chunks, _, width = e1.shape
    trades = price.shape[2]
    sources = q0.shape[0]
    blocks, _, _ = pk0.shape
    step = sources // blocks
    near = sources // 2
    group = 2 * lax.div(r, 2) + lax.rem(c, 2)

    def row_peer(m):
        return (flip(r, m, rows), c)

    def col_peer(s):
        return (r, flip(c, s, cols))

    def line_peer(m):
        return (flip(r, m - m % 2, rows), flip(c, m % 2, cols))

    def plane_peer(s):
        return (flip(r, s % 2, rows), flip(c, s - s % 2, cols))

    def remote(src, dst, send, recv, peer):
        return pltpu.make_async_remote_copy(
            src_ref=src, dst_ref=dst, send_sem=send, recv_sem=recv, device_id=peer, device_id_type=MESH
        )

    beside = [col_peer(s) for s in range(1, cols)]
    m = 1
    while m < rows:
        beside.append(row_peer(m))
        m *= 2
    barrier = pltpu.get_barrier_semaphore()

    def call(sem):
        for peer in beside:
            pl.semaphore_signal(sem, inc=1, device_id=peer, device_id_type=MESH)

    call(barrier)
    loads = [
        pltpu.make_async_copy(a, b, local.at[i])
        for i, (a, b) in enumerate(
            [
                (n1_hbm, n1_ref),
                (precision_hbm, precision_ref),
                (drift_hbm, drift_ref),
                (n2_hbm, n2_ref),
                (nz_hbm, nz_ref),
                (terminal_hbm, terminal_ref),
                (ex1_hbm, ex1_ref),
                (flags_hbm, flags_ref),
                (ex0_hbm, ex0_ref),
            ]
        )
    ]
    for load in loads:
        load.start()
    for load in loads[:3]:
        load.wait()
    precision = column_of(precision_ref[...])
    drift = column_of(drift_ref[...])
    mine = queries_of(n1_ref[...], precision, drift, height)
    q1t[0] = mine.astype(jnp.bfloat16)
    t1[0, :depth, :] = n1_ref[...].astype(jnp.bfloat16)
    pl.semaphore_wait(barrier, len(beside))
    call(ready.at[0])

    def q_copy(s):
        return remote(q1t.at[0], q1t.at[s], q_send.at[0], q_recv.at[s - 1], col_peer(s))

    far = list(range(2, cols, 2)) + list(range(3, cols, 2))
    for s in [1] + far:
        q_copy(s).start()

    def t_copy(m):
        if m % 2:
            src, peer = t1.at[m - 1, pl.ds(0, depth)], col_peer(1)
        else:
            src, peer = t1.at[0, pl.ds(0, depth)], row_peer(m)
        return remote(src, t1.at[m, pl.ds(0, depth)], t_send.at[0], t_recv.at[m % 2], peer)

    t_copy(1).start()
    soon = [m for m in range(2, rows, 2) if m & (m - 1) == 0]
    late = [m for m in range(2, rows, 2) if m & (m - 1)]
    for m in soon:
        t_copy(m).start()

    q1[0] = upright(mine, lanes)
    for m in range(rows):
        t1[m, depth:, :] = ones_under(lanes - depth, own)
    loads[3].wait()
    for k in range(chunks):
        t2[k, :depth, :] = n2_ref[:, k * width : (k + 1) * width].astype(jnp.bfloat16)
        t2[k, depth:, :] = ones_under(lanes - depth, width)

    def stats_one(s):
        for k in range(chunks):
            x, peak, total = scored(q1[s], t2[k])
            e1[s, k] = x
            pk1[s, k : k + 1, :] = peak
            tt1[s, k : k + 1, :] = total

    def stats_zero(m, first, last):
        row = flip(group, m, rows)
        for b in range(first, last):
            x, peak, total = scored(q0[b * step : (b + 1) * step, :], t1[m])
            e0[m, b * step : (b + 1) * step, :] = x
            pk0[b, pl.ds(row, 1), :] = peak
            tt0[b, pl.ds(row, 1), :] = total

    def take_q(s):
        q_copy(s).wait_recv()
        q1[s] = upright(q1t[s].astype(jnp.float32), lanes)

    stats_one(0)
    loads[4].wait()
    q0a[...] = upright(queries_of(nz_ref[...], precision, drift, height), lanes)
    for s in range(0, cols, 2):
        at = pl.multiple_of(flip(c, s, cols) * own, own)
        q0[s // 2 * own : (s // 2 + 1) * own, :] = q0a[pl.ds(at, own), :]
    y_copy = remote(q0.at[pl.ds(0, near)], q0.at[pl.ds(near, near)], y_send.at[0], y_recv.at[0], row_peer(1))
    y_copy.start()
    take_q(1)
    stats_one(1)
    rounds = ready.shape[0]

    def hear(i):
        pl.semaphore_wait(ready.at[i], len(beside))
        if i + 1 < rounds:
            call(ready.at[i + 1])

    hear(0)
    for m in late:
        t_copy(m).start()
    stats_zero(0, 0, blocks // 2)
    for s in far:
        take_q(s)
        stats_one(s)

    def l1_copy(m):
        return remote(l1.at[0], l1.at[m], l1_send.at[0], l1_recv.at[0], row_peer(m))

    for i in range(1, rounds):
        hear(i)
    l1[0] = merged([pk1[s] for s in range(cols)], [tt1[s] for s in range(cols)])
    for m in reversed(range(1, rows)):
        l1_copy(m).start()

    def t_all(first, count):
        view = t1.at[pl.ds(first, count), pl.ds(0, depth)]
        return remote(view, view, t_send.at[0], t_recv.at[first % 2], col_peer(1))

    if rows > 2:
        t_all(2, rows // 2 - 1).wait_recv()
    for m in range(2, rows, 2):
        t_copy(m + 1).start()
    y_copy.wait_recv()
    stats_zero(0, blocks // 2, blocks)
    for m in range(2, rows, 2):
        stats_zero(m, 0, blocks)
    t_all(1, rows // 2).wait_recv()
    for m in range(1, rows, 2):
        stats_zero(m, 0, blocks)
    l0[0] = merged([pk0[b] for b in range(blocks)], [tt0[b] for b in range(blocks)])

    def l0_copy(m):
        return remote(l0.at[0], l0.at[m], l0_send.at[0], l0_recv.at[0], line_peer(m))

    for m in reversed(range(1, rows)):
        l0_copy(m).start()

    def weights_one(s, k):
        return (e1[s, k] * f1[s, k : k + 1, :]).astype(jnp.bfloat16)

    def partial_one(s):
        total = None
        for k in range(chunks):
            part = jnp.dot(
                weights_one(s, k), terminal_ref[k * width : (k + 1) * width, :], preferred_element_type=jnp.float32
            )
            total = part if total is None else total + part
        return total

    def pair_copy(out, into, send, recv, s):
        return remote(out.at[s // 2], into.at[s // 2], send.at[0], recv.at[s // 2], col_peer(1))

    def far_copy(s, h):
        at = h * (cols // 2 - 1) + s // 2 - 1
        piece = pl.ds(h * size, size)
        return remote(
            far_out1.at[s // 2, piece], far_in1.at[s // 2, piece], far1_send.at[0], far1_recv.at[at], col_peer(s)
        )

    def last_copy(s, h):
        piece = pl.ds(h * count, count)
        return remote(far_out0.at[s, piece], far_in0.at[s, piece], far0_send.at[0], far0_recv.at[h], plane_peer(s))

    pair1 = (pair_out1, pair_in1, pair1_send, pair1_recv)
    size = own // PARTS
    count = own // LAST
    away = list(range(2, cols, 2))

    l1_all = remote(l1.at[pl.ds(1, rows - 1)], l1.at[pl.ds(1, rows - 1)], l1_send.at[0], l1_recv.at[0], row_peer(1))
    l1_all.wait_recv()
    loads[5].wait()
    level = merged([l1[m] for m in range(rows)], None)
    for s in range(cols):
        f1[s] = jnp.exp(pk1[s] - level)
    for s in [s + 1 for s in away] + [1] + away + [0]:
        total = partial_one(s)
        if s % 2:
            pair_out1[s // 2] = total
            pair_copy(*pair1, s - 1).start()
        else:
            acc1[s // 2] = total
    for s in away:
        pair_copy(*pair1, s).wait_recv()
        for h in range(PARTS):
            piece = slice(h * size, (h + 1) * size)
            far_out1[s // 2, piece, :] = acc1[s // 2, piece, :] + pair_in1[s // 2, piece, :]
            far_copy(s, h).start()
    pair_copy(*pair1, 0).wait_recv()
    held = acc1[0] + pair_in1[0]
    loads[6].wait()
    loads[7].wait()
    l0_all = remote(l0.at[pl.ds(1, rows - 1)], l0.at[pl.ds(1, rows - 1)], l0_send.at[0], l0_recv.at[0], col_peer(1))
    l0_all.wait_recv()
    level = merged([l0[m] for m in range(rows)], None)
    for b in range(blocks):
        f0[b] = jnp.exp(pk0[b] - level)

    def p_copy(m, h):
        piece = pl.ds(h * size, size)
        if m % 2:
            src, peer, recv = price.at[m - 1, piece], col_peer(1), pc_recv.at[m // 2]
        else:
            recv = p_recv.at[h * (rows // 2 - 1) + m // 2 - 1]
            src, peer = (price.at[m - 2, piece], row_peer(2)) if relayed(m, h) else (price.at[0, piece], row_peer(m))
        return remote(src, price.at[m, piece], p_send.at[0], recv, peer)

    def relayed(m, h):
        return h < RELAY and m % 4 == 2 and m > 2

    def p_core(m):
        return remote(price.at[m], price.at[m], p_send.at[0], pc_recv.at[m // 2], col_peer(1))

    for h in range(PARTS):
        piece = slice(h * size, (h + 1) * size)
        carried = held[piece]
        for s in away:
            far_copy(s, h).wait_recv()
            carried = carried + far_in1[s // 2, piece, :]
        value = settled(flags_ref[1:2, :], ex1_ref[piece, :], carried)
        price[0, piece, :] = value.astype(jnp.bfloat16)
        for m in range(rows - 2, 0, -2):
            if not relayed(m, h):
                p_copy(m, h).start()
        p_copy(1, h).start()
        v1_ref[piece, :] = value
    keep_one = pltpu.make_async_copy(v1_ref, v1_out, local.at[9])
    keep_one.start()

    def add_zero(m, first, count):
        row = flip(group, m, rows)
        parts = []
        each = min(step, count)
        for at in range(first, first + count, each):
            w = (e0[m, at : at + each, :] * f0[at // step, pl.ds(row, 1), :]).astype(jnp.bfloat16)
            parts.append(jnp.dot(w, price[m], preferred_element_type=jnp.float32))
        return parts[0] if len(parts) == 1 else jnp.concatenate(parts, axis=0)

    def gain(m):
        for at in range(0, sources, step):
            part = add_zero(m, at, step)
            acc0[at : at + step, :] = part if m == 0 else acc0[at : at + step, :] + part

    gain(0)
    def pass_on(m, h):
        p_copy(m, h).wait_recv()
        if m + 2 < rows and relayed(m + 2, h) and m % 4 == 0:
            p_copy(m + 2, h).start()
        p_copy(m + 1, h).start()

    direct = [m for m in range(2, rows, 2) if m % 4 == 0 or m == 2]
    other = [m for m in range(2, rows, 2) if m not in direct]
    for h in range(PARTS):
        for m in reversed(direct):
            pass_on(m, h)
        for m in other:
            if not relayed(m, h):
                pass_on(m, h)
    p_core(1).wait_recv()
    for m in [1] + direct:
        gain(m)
    for h in range(min(RELAY, PARTS)):
        for m in other:
            pass_on(m, h)
    for m in other:
        gain(m)
    for m in range(3, rows - 2, 2):
        p_core(m).wait_recv()
        gain(m)
    if rows > 2:
        p_core(rows - 1).wait_recv()
    held = None
    for s in [s + 1 for s in away] + away + [1, 0]:
        at = (s % 2) * near + s // 2 * own
        total = acc0[at : at + own, :] + add_zero(rows - 1, at, own)
        if s:
            far_out0[s] = total.astype(far_out0.dtype)
            for h in range(LAST):
                last_copy(s, h).start()
        else:
            held = total
    loads[8].wait()
    for h in range(LAST):
        piece = slice(h * count, (h + 1) * count)
        carried = held[piece]
        view = far_in0.at[pl.ds(1, cols - 1), pl.ds(h * count, count)]
        remote(view, view, far0_send.at[0], far0_recv.at[h], col_peer(1)).wait_recv()
        for s in range(1, cols):
            carried = carried + far_in0[s, piece, :].astype(jnp.float32)
        v0_ref[piece, :] = settled(flags_ref[0:1, :], ex0_ref[piece, :], carried)
    keep_zero = pltpu.make_async_copy(v0_ref, v0_out, local.at[10])
    keep_zero.start()

    y_copy.wait_send()

    def sent(ref, first, count, sem):
        view = ref.at[pl.ds(first, count)]
        remote(view, view, sem.at[0], y_recv.at[0], col_peer(1)).wait_send()

    sent(q1t, 0, cols - 1, q_send)
    t_all(1, rows - 1).wait_send()
    l1_all.wait_send()
    l0_all.wait_send()
    sent(price, 0, rows - 1, p_send)
    sent(pair_out1, 0, cols // 2, pair1_send)
    if away:
        sent(far_out1, 1, cols // 2 - 1, far1_send)
    sent(far_out0, 1, cols - 1, far0_send)
    keep_one.wait()
    keep_zero.wait()


def shards(rows, cols, nodes_zero, nodes_one, nodes_two, precision, drift, terminal, ex1, ex0, flags):
    own, depth = nodes_one.shape
    height = depth + 16
    sources = nodes_zero.shape[0]
    targets = nodes_two.shape[0]
    trades = terminal.shape[1]
    width = min(TILE, targets)
    chunks = targets // width
    step = max(own, min(TILE, sources))
    blocks = sources // step
    lanes = 128 * (-(-(depth + 3) // 128))
    dma = pltpu.SemaphoreType.DMA
    f32, bf16 = jnp.float32, jnp.bfloat16
    row_stat = pltpu.VMEM((cols, chunks, width), f32)
    col_stat = pltpu.VMEM((blocks, rows, own), f32)
    piece = pltpu.VMEM((cols // 2, own, trades), f32)
    slim = pltpu.VMEM((cols, own, trades), bf16)
    mine = pltpu.VMEM((own, trades), f32)
    one, zero = pl.pallas_call(
        functools.partial(body, rows, cols),
        out_shape=(pltpu.VMEM((own, trades), f32),) * 2,
        in_specs=[pl.BlockSpec(memory_space=pltpu.HBM)] * 9,
        out_specs=(pl.BlockSpec(memory_space=pl.ANY),) * 2,
        scratch_shapes=[
            pltpu.VMEM((1, depth), f32),
            pltpu.VMEM((1, depth), f32),
            pltpu.VMEM((2, trades), jnp.int32),
            pltpu.VMEM((depth, sources), f32),
            pltpu.VMEM((depth, own), f32),
            pltpu.VMEM((depth, targets), f32),
            pltpu.VMEM((targets, trades), bf16),
            *[mine] * 4,
            pltpu.VMEM((cols, height, own), bf16),
            pltpu.VMEM((cols, own, lanes), bf16),
            pltpu.VMEM((rows, lanes, own), bf16),
            pltpu.VMEM((sources, lanes), bf16),
            pltpu.VMEM((sources, lanes), bf16),
            pltpu.VMEM((chunks, lanes, width), bf16),
            pltpu.VMEM((cols, chunks, own, width), f32),
            pltpu.VMEM((rows, sources, own), f32),
            row_stat,
            row_stat,
            row_stat,
            col_stat,
            col_stat,
            col_stat,
            pltpu.VMEM((rows, chunks, width), f32),
            pltpu.VMEM((rows, rows, own), f32),
            pltpu.VMEM((rows, own, trades), bf16),
            piece,
            pltpu.VMEM((sources, trades), f32),
            *[piece] * 4,
            *[slim] * 2,
            dma((1,)),
            dma((cols - 1,)),
            dma((1,)),
            dma((2,)),
            *[dma((1,))] * 5,
            dma((PARTS * max(1, rows // 2 - 1),)),
            dma((rows // 2,)),
            dma((1,)),
            dma((cols // 2,)),
            dma((1,)),
            dma((PARTS * max(1, cols // 2 - 1),)),
            *[dma((1,))] * 3,
            dma((LAST,)),
            dma((11,)),
            pltpu.SemaphoreType.REGULAR((max(1, rows.bit_length() - 2),)),
        ],
        compiler_params=pltpu.CompilerParams(
            collective_id=0, has_side_effects=True, vmem_limit_bytes=LIMIT
        ),
    )(nodes_zero.T, nodes_one.T, nodes_two.T, precision[None, :], drift[None, :], terminal, ex1, ex0, flags)
    return handed(one, zero)


def hand(a, b, c, d, sems):
    copies = [pltpu.make_async_copy(a, c, sems.at[0]), pltpu.make_async_copy(b, d, sems.at[1])]
    for copy in copies:
        copy.start()
    for copy in copies:
        copy.wait()


def handed(one, zero):
    here = pl.BlockSpec(memory_space=pltpu.VMEM)
    out = jax.ShapeDtypeStruct(one.shape, one.dtype)
    return pl.pallas_call(
        hand,
        out_shape=(out, out),
        in_specs=[here, here],
        out_specs=(pl.BlockSpec(memory_space=pltpu.HBM),) * 2,
        scratch_shapes=[pltpu.SemaphoreType.DMA((2,))],
        compiler_params=pltpu.CompilerParams(vmem_limit_bytes=2 * 1024 * 1024),
    )(one, zero)


def solution(mesh):
    both = P(("row", "col"), None)
    return jax.shard_map(
        functools.partial(shards, mesh.shape["row"], mesh.shape["col"]),
        mesh=mesh,
        in_specs=(P("row", None), both, P("col", None), P(), P(), P("col", None), both, both, P()),
        out_specs=(both, both),
        check_vma=False,
    )
```

```python
import functools

import jax
import jax.numpy as jnp
from jax import lax
from jax.experimental import pallas as pl
from jax.experimental.pallas import tpu as pltpu
from jax.sharding import PartitionSpec as P

MESH = pl.DeviceIdType.MESH
TILE = 256
PARTS = 4
RELAY = 2
CUTS = 2
LAST = 2
LIMIT = 60 * 1024 * 1024


def flip(index, mask, size):
    bit = 1
    while bit < size:
        if mask & bit:
            index = index + bit - 2 * bit * lax.rem(lax.div(index, bit), 2)
        bit *= 2
    return index


def column_of(row):
    return jnp.broadcast_to(row, (128, row.shape[1])).T[:, :1]


def queries_of(nodes, precision, drift, height):
    shifted = nodes + drift
    offsets = 0.5 * jnp.sum(precision * shifted * shifted, axis=0, keepdims=True)
    first = offsets.astype(jnp.bfloat16).astype(jnp.float32)
    rest = offsets - first
    second = rest.astype(jnp.bfloat16).astype(jnp.float32)
    third = rest - second
    count = height - nodes.shape[0]
    at = lax.broadcasted_iota(jnp.int32, (count, nodes.shape[1]), 0)
    extra = jnp.where(at == 0, first, jnp.where(at == 1, second, jnp.where(at == 2, third, 0.0)))
    return jnp.concatenate([shifted * precision, extra], axis=0)


def upright(tall, lanes):
    short = lanes - tall.shape[0]
    if short:
        tall = jnp.concatenate([tall, jnp.zeros((short, tall.shape[1]), tall.dtype)], axis=0)
    return tall.T.astype(jnp.bfloat16)


def ones_under(count, width):
    at = lax.broadcasted_iota(jnp.int32, (count, width), 0)
    return jnp.where(at < 3, -1.0, 0.0).astype(jnp.bfloat16)


def settled(allowed, exercise, carried):
    return jnp.where(allowed == 1, jnp.maximum(exercise, carried), carried)


def scored(queries, targets):
    s = lax.dot_general(queries, targets, (((1,), (0,)), ((), ())), preferred_element_type=jnp.float32)
    fold = (s.shape[0] // 8, 8, s.shape[1])
    peak = jnp.max(jnp.max(s.reshape(fold), axis=0), axis=0, keepdims=True)
    x = jnp.exp(s - peak)
    return x, peak, jnp.sum(jnp.sum(x.reshape(fold), axis=0), axis=0, keepdims=True)


def merged(levels, totals):
    top = functools.reduce(jnp.maximum, levels)
    total = None
    for i, level in enumerate(levels):
        term = jnp.exp(level - top)
        if totals is not None:
            term = totals[i] * term
        total = term if total is None else total + term
    return top + jnp.log(total)


def body(
    rows,
    cols,
    nz_hbm,
    n1_hbm,
    n2_hbm,
    precision_hbm,
    drift_hbm,
    terminal_hbm,
    ex1_hbm,
    ex0_hbm,
    flags_hbm,
    v1_out,
    v0_out,
    precision_ref,
    drift_ref,
    flags_ref,
    nz_ref,
    n1_ref,
    n2_ref,
    terminal_ref,
    ex1_ref,
    ex0_ref,
    v1_ref,
    v0_ref,
    q1t,
    q1,
    t1,
    q0a,
    q0,
    t2,
    e1,
    e0,
    pk1,
    tt1,
    f1,
    pk0,
    tt0,
    f0,
    l1,
    l0,
    price,
    acc1,
    acc0,
    pair_out1,
    pair_in1,
    far_out1,
    far_in1,
    far_out0,
    far_in0,
    q_send,
    q_recv,
    t_send,
    t_recv,
    l1_send,
    l1_recv,
    l0_send,
    l0_recv,
    p_send,
    p_recv,
    pc_recv,
    pair1_send,
    pair1_recv,
    far1_send,
    far1_recv,
    y_send,
    y_recv,
    far0_send,
    far0_recv,
    local,
    ready,
):
    r = lax.axis_index("row")
    c = lax.axis_index("col")
    depth, own = n1_ref.shape
    lanes = q0.shape[1]
    height = q1t.shape[1]
    _, chunks, _, width = e1.shape
    trades = price.shape[2]
    sources = q0.shape[0]
    blocks, _, _ = pk0.shape
    step = sources // blocks
    near = sources // 2
    group = 2 * lax.div(r, 2) + lax.rem(c, 2)

    def row_peer(m):
        return (flip(r, m, rows), c)

    def col_peer(s):
        return (r, flip(c, s, cols))

    def line_peer(m):
        return (flip(r, m - m % 2, rows), flip(c, m % 2, cols))

    def plane_peer(s):
        return (flip(r, s % 2, rows), flip(c, s - s % 2, cols))

    def remote(src, dst, send, recv, peer):
        return pltpu.make_async_remote_copy(
            src_ref=src, dst_ref=dst, send_sem=send, recv_sem=recv, device_id=peer, device_id_type=MESH
        )

    line = rows // 2
    deep = lax.div(r, 2)
    core = lax.rem(c, 2)
    beside = cols + jnp.where(deep > 0, 1, 0) + jnp.where(deep < line - 1, 1, 0)
    barrier = pltpu.get_barrier_semaphore()

    def call(sem):
        for s in range(1, cols):
            pl.semaphore_signal(sem, inc=1, device_id=col_peer(s), device_id_type=MESH)
        pl.semaphore_signal(sem, inc=1, device_id=row_peer(1), device_id_type=MESH)

        @pl.when(deep > 0)
        def _():
            pl.semaphore_signal(sem, inc=1, device_id=(r - 2, c), device_id_type=MESH)

        @pl.when(deep < line - 1)
        def _():
            pl.semaphore_signal(sem, inc=1, device_id=(r + 2, c), device_id_type=MESH)

    call(barrier)
    loads = [
        pltpu.make_async_copy(a, b, local.at[i])
        for i, (a, b) in enumerate(
            [
                (n1_hbm, n1_ref),
                (precision_hbm, precision_ref),
                (drift_hbm, drift_ref),
                (n2_hbm, n2_ref),
                (nz_hbm, nz_ref),
                (terminal_hbm, terminal_ref),
                (ex1_hbm, ex1_ref),
                (flags_hbm, flags_ref),
                (ex0_hbm, ex0_ref),
            ]
        )
    ]
    for load in loads:
        load.start()
    for load in loads[:3]:
        load.wait()
    precision = column_of(precision_ref[...])
    drift = column_of(drift_ref[...])
    mine = queries_of(n1_ref[...], precision, drift, height)
    q1t[0] = mine.astype(jnp.bfloat16)
    t1[0, :depth, :] = n1_ref[...].astype(jnp.bfloat16)
    pl.semaphore_wait(barrier, beside)
    call(ready.at[0])

    def q_copy(s, peer):
        return remote(q1t.at[0], q1t.at[s], q_send.at[0], q_recv.at[s - 1], peer)

    q_copy(1, col_peer(1)).start()
    for other in range(2):
        for s in range(2, cols, 2):
            slot = s + (1 - core if other else core)
            q_copy(slot, (r, flip(c, s, cols) - core + other)).start()

    def t_copy(m):
        if m % 2:
            src, peer = t1.at[m - 1, pl.ds(0, depth)], col_peer(1)
        else:
            src, peer = t1.at[0, pl.ds(0, depth)], row_peer(m)
        return remote(src, t1.at[m, pl.ds(0, depth)], t_send.at[0], t_recv.at[m % 2 + (2 if m >= 6 else 0)], peer)

    t_copy(1).start()
    if rows > 2:
        t_copy(2).start()

    q1[0] = upright(mine, lanes)
    for m in range(rows):
        t1[m, depth:, :] = ones_under(lanes - depth, own)
    loads[3].wait()
    for k in range(chunks):
        t2[k, :depth, :] = n2_ref[:, k * width : (k + 1) * width].astype(jnp.bfloat16)
        t2[k, depth:, :] = ones_under(lanes - depth, width)

    def stats_one(s):
        for k in range(chunks):
            x, peak, total = scored(q1[s], t2[k])
            e1[s, k] = x
            pk1[s, pl.ds(k, 1), :] = peak
            tt1[s, pl.ds(k, 1), :] = total

    def stats_zero(m, first, last):
        row = flip(group, m, rows)
        for b in range(first, last):
            x, peak, total = scored(q0[b * step : (b + 1) * step, :], t1[m])
            e0[m, b * step : (b + 1) * step, :] = x
            pk0[b, pl.ds(row, 1), :] = peak
            tt0[b, pl.ds(row, 1), :] = total

    def take_q(s):
        q_copy(s, col_peer(1)).wait_recv()
        q1[s] = upright(q1t[s].astype(jnp.float32), lanes)

    stats_one(0)
    loads[4].wait()
    q0a[...] = upright(queries_of(nz_ref[...], precision, drift, height), lanes)
    for s in range(0, cols, 2):
        at = pl.multiple_of(flip(c, s, cols) * own, own)
        q0[s // 2 * own : (s // 2 + 1) * own, :] = q0a[pl.ds(at, own), :]
    y_copy = remote(q0.at[pl.ds(0, near)], q0.at[pl.ds(near, near)], y_send.at[0], y_recv.at[0], row_peer(1))
    y_copy.start()
    rounds = ready.shape[0]

    def hear(i):
        pl.semaphore_wait(ready.at[i], beside)
        if i + 1 < rounds:
            call(ready.at[i + 1])

    take_q(1)
    stats_one(1)
    stats_zero(0, 0, blocks // 2)
    hear(0)
    if rows > 4:
        t_copy(4).start()
    for other in range(2):
        for s in range(2, cols, 2):
            slot = s + (core if other else 1 - core)
            take_q(slot)
            stats_one(slot)
        if other == 0:
            for i in range(1, rounds - 1):
                hear(i)
            for m in range(6, rows, 2):
                t_copy(m).start()

    def l1_copy(m):
        return remote(l1.at[0], l1.at[m], l1_send.at[0], l1_recv.at[0], row_peer(m))

    if rounds > 1:
        hear(rounds - 1)
    l1[0] = merged([pk1[s] for s in range(cols)], [tt1[s] for s in range(cols)])
    for m in reversed(range(1, rows)):
        l1_copy(m).start()

    def t_all(count, at):
        view = t1.at[pl.ds(0, count), pl.ds(0, depth)]
        return remote(view, view, t_send.at[0], t_recv.at[at], col_peer(1))

    first_ones, late_ones = range(2, min(6, rows), 2), range(6, rows, 2)
    if first_ones:
        t_all(len(first_ones), 0).wait_recv()
        for m in first_ones:
            t_copy(m + 1).start()
    y_copy.wait_recv()
    stats_zero(0, blocks // 2, blocks)
    for m in first_ones:
        stats_zero(m, 0, blocks)
    t_all(1 + len(first_ones), 1).wait_recv()
    if late_ones:
        t_all(len(late_ones), 2).wait_recv()
        for m in late_ones:
            t_copy(m + 1).start()
    for m in [1] + [m + 1 for m in first_ones]:
        stats_zero(m, 0, blocks)

    def weights_one(s, k, first, many):
        return (e1[s, k, first : first + many, :] * f1[s, k : k + 1, :]).astype(jnp.bfloat16)

    def partial_one(s, first, many):
        total = None
        for k in range(chunks):
            part = jnp.dot(
                weights_one(s, k, first, many), terminal_ref[k * width : (k + 1) * width, :], preferred_element_type=jnp.float32
            )
            total = part if total is None else total + part
        return total

    cut = own // CUTS

    def pair_copy(s, h):
        piece = pl.ds(h * cut, cut)
        at = h * (cols // 2) + s // 2
        return remote(
            pair_out1.at[s // 2, piece], pair_in1.at[s // 2, piece], pair1_send.at[0], pair1_recv.at[at], col_peer(1)
        )

    def far_copy(s, h):
        at = h * (cols // 2 - 1) + s // 2 - 1
        piece = pl.ds(h * size, size)
        return remote(
            far_out1.at[s // 2, piece], far_in1.at[s // 2, piece], far1_send.at[0], far1_recv.at[at], col_peer(s)
        )

    def last_copy(s, h):
        piece = pl.ds(h * count, count)
        return remote(far_out0.at[s, piece], far_in0.at[s, piece], far0_send.at[0], far0_recv.at[h], plane_peer(s))

    size = own // PARTS
    count = own // LAST
    away = list(range(2, cols, 2))

    l1_all = remote(l1.at[pl.ds(1, rows - 1)], l1.at[pl.ds(1, rows - 1)], l1_send.at[0], l1_recv.at[0], row_peer(1))
    l1_all.wait_recv()
    loads[5].wait()
    level = merged([l1[m] for m in range(rows)], None)
    for s in range(cols):
        f1[s] = jnp.exp(pk1[s] - level)
    def give(s):
        for h in range(CUTS):
            pair_out1[s // 2, h * cut : (h + 1) * cut, :] = partial_one(s + 1, h * cut, cut)
            pair_copy(s, h).start()

    for s in away:
        give(s)
    for s in away:
        acc1[s // 2] = partial_one(s, 0, own)
    give(0)
    for h in range(CUTS):
        for s in away:
            pair_copy(s, h).wait_recv()
            for i in range(h * PARTS // CUTS, (h + 1) * PARTS // CUTS):
                piece = slice(i * size, (i + 1) * size)
                far_out1[s // 2, piece, :] = acc1[s // 2, piece, :] + pair_in1[s // 2, piece, :]
                far_copy(s, i).start()
    acc1[0] = partial_one(0, 0, own)
    for h in range(CUTS):
        pair_copy(0, h).wait_recv()
    held = acc1[0] + pair_in1[0]
    for m in late_ones:
        stats_zero(m, 0, blocks)
    if late_ones:
        t_all(len(late_ones), 3).wait_recv()
    for m in late_ones:
        stats_zero(m + 1, 0, blocks)
    l0[0] = merged([pk0[b] for b in range(blocks)], [tt0[b] for b in range(blocks)])

    def l0_copy(m):
        return remote(l0.at[0], l0.at[m], l0_send.at[0], l0_recv.at[0], line_peer(m))

    for m in reversed(range(1, rows)):
        l0_copy(m).start()

    loads[6].wait()
    loads[7].wait()

    def p_copy(m, h):
        piece = pl.ds(h * size, size)
        if m % 2:
            src, peer, recv = price.at[m - 1, piece], col_peer(1), pc_recv.at[m // 2]
        else:
            recv = p_recv.at[h * (rows // 2 - 1) + m // 2 - 1]
            src, peer = (price.at[m - 2, piece], row_peer(2)) if relayed(m, h) else (price.at[0, piece], row_peer(m))
        return remote(src, price.at[m, piece], p_send.at[0], recv, peer)

    def relayed(m, h):
        return h < RELAY and m % 4 == 2 and m > 2

    def p_core(m):
        return remote(price.at[m], price.at[m], p_send.at[0], pc_recv.at[m // 2], col_peer(1))

    for h in range(PARTS):
        piece = slice(h * size, (h + 1) * size)
        carried = held[piece]
        for s in away:
            far_copy(s, h).wait_recv()
            carried = carried + far_in1[s // 2, piece, :]
        value = settled(flags_ref[1:2, :], ex1_ref[piece, :], carried)
        price[0, piece, :] = value.astype(jnp.bfloat16)
        for m in range(rows - 2, 0, -2):
            if not relayed(m, h):
                p_copy(m, h).start()
        p_copy(1, h).start()
        v1_ref[piece, :] = value
    keep_one = pltpu.make_async_copy(v1_ref, v1_out, local.at[9])
    keep_one.start()
    def add_zero(m, row, first, count):
        parts = []
        each = min(step, count)
        for at in range(first, first + count, each):
            w = (e0[m, at : at + each, :] * f0[at // step, pl.ds(row, 1), :]).astype(jnp.bfloat16)
            parts.append(jnp.dot(w, price[m], preferred_element_type=jnp.float32))
        return parts[0] if len(parts) == 1 else jnp.concatenate(parts, axis=0)

    def gain(slots):
        for at in range(0, sources, step):
            total = acc0[at : at + step, :] if 0 not in slots else None
            for m in slots:
                part = add_zero(m, flip(group, m, rows), at, step)
                total = part if total is None else total + part
            acc0[at : at + step, :] = total

    def pass_on(m, h):
        p_copy(m, h).wait_recv()
        if m + 2 < rows and relayed(m + 2, h) and m % 4 == 0:
            p_copy(m + 2, h).start()
        p_copy(m + 1, h).start()

    def ready_zero():
        l0_all = remote(l0.at[pl.ds(1, rows - 1)], l0.at[pl.ds(1, rows - 1)], l0_send.at[0], l0_recv.at[0], col_peer(1))
        l0_all.wait_recv()
        level = merged([l0[m] for m in range(rows)], None)
        for b in range(blocks):
            f0[b] = jnp.exp(pk0[b] - level)

    direct = [m for m in range(2, rows, 2) if m % 4 == 0 or m == 2]
    other = [m for m in range(2, rows, 2) if m not in direct]
    for h in range(PARTS):
        for m in reversed(direct):
            pass_on(m, h)
        for m in other:
            if not relayed(m, h):
                pass_on(m, h)
        if h == PARTS // 2 - 1:
            ready_zero()
            p_core(1).wait_recv()
            gain([0, 1])
    gain(direct)
    for h in range(min(RELAY, PARTS)):
        for m in other:
            pass_on(m, h)
    ahead = [m for m in range(3, rows - 2, 2)]
    for m in ahead:
        p_core(m).wait_recv()
    if ahead:
        gain(ahead)

    @pl.when(core == 0)
    def _():
        if rows > 2:
            p_core(rows - 1).wait_recv()
        if other:
            gain(other[:-1] + [rows - 1])

    @pl.when(core == 1)
    def _():
        if other:
            gain(other)
        if rows > 2:
            p_core(rows - 1).wait_recv()

    if other:
        final, final_row = rows - 2 + core, flip(group, rows - 2, rows) - core
    else:
        final, final_row = rows - 1, flip(group, rows - 1, rows)
    held = None
    for s in [s + 1 for s in away] + away + [1, 0]:
        at = (s % 2) * near + s // 2 * own
        total = acc0[at : at + own, :] + add_zero(final, final_row, at, own)
        if s:
            far_out0[s] = total.astype(far_out0.dtype)
            for h in range(LAST):
                last_copy(s, h).start()
        else:
            held = total
    loads[8].wait()
    for h in range(LAST):
        piece = slice(h * count, (h + 1) * count)
        carried = held[piece]
        view = far_in0.at[pl.ds(1, cols - 1), pl.ds(h * count, count)]
        remote(view, view, far0_send.at[0], far0_recv.at[h], col_peer(1)).wait_recv()
        for s in range(1, cols):
            carried = carried + far_in0[s, piece, :].astype(jnp.float32)
        v0_ref[piece, :] = settled(flags_ref[0:1, :], ex0_ref[piece, :], carried)
    keep_zero = pltpu.make_async_copy(v0_ref, v0_out, local.at[10])
    keep_zero.start()

    y_copy.wait_send()

    def sent(ref, first, count, sem):
        view = ref.at[pl.ds(first, count)]
        remote(view, view, sem.at[0], y_recv.at[0], col_peer(1)).wait_send()

    sent(q1t, 0, cols - 1, q_send)
    t_all(rows - 1, 0).wait_send()
    l1_all.wait_send()
    remote(l0.at[pl.ds(1, rows - 1)], l0.at[pl.ds(1, rows - 1)], l0_send.at[0], l0_recv.at[0], col_peer(1)).wait_send()
    sent(price, 0, rows - 1, p_send)
    sent(pair_out1, 0, cols // 2, pair1_send)
    if away:
        sent(far_out1, 1, cols // 2 - 1, far1_send)
    sent(far_out0, 1, cols - 1, far0_send)
    keep_one.wait()
    keep_zero.wait()


def shards(rows, cols, nodes_zero, nodes_one, nodes_two, precision, drift, terminal, ex1, ex0, flags):
    own, depth = nodes_one.shape
    height = depth + 16
    sources = nodes_zero.shape[0]
    targets = nodes_two.shape[0]
    trades = terminal.shape[1]
    width = min(TILE, targets)
    chunks = targets // width
    step = max(own, min(TILE, sources))
    blocks = sources // step
    lanes = 128 * (-(-(depth + 3) // 128))
    dma = pltpu.SemaphoreType.DMA
    f32, bf16 = jnp.float32, jnp.bfloat16
    row_stat = pltpu.VMEM((cols, chunks, width), f32)
    col_stat = pltpu.VMEM((blocks, rows, own), f32)
    piece = pltpu.VMEM((cols // 2, own, trades), f32)
    slim = pltpu.VMEM((cols, own, trades), bf16)
    mine = pltpu.VMEM((own, trades), f32)
    one, zero = pl.pallas_call(
        functools.partial(body, rows, cols),
        out_shape=(pltpu.VMEM((own, trades), f32),) * 2,
        in_specs=[pl.BlockSpec(memory_space=pltpu.HBM)] * 9,
        out_specs=(pl.BlockSpec(memory_space=pl.ANY),) * 2,
        scratch_shapes=[
            pltpu.VMEM((1, depth), f32),
            pltpu.VMEM((1, depth), f32),
            pltpu.VMEM((2, trades), jnp.int32),
            pltpu.VMEM((depth, sources), f32),
            pltpu.VMEM((depth, own), f32),
            pltpu.VMEM((depth, targets), f32),
            pltpu.VMEM((targets, trades), bf16),
            *[mine] * 4,
            pltpu.VMEM((cols, height, own), bf16),
            pltpu.VMEM((cols, own, lanes), bf16),
            pltpu.VMEM((rows, lanes, own), bf16),
            pltpu.VMEM((sources, lanes), bf16),
            pltpu.VMEM((sources, lanes), bf16),
            pltpu.VMEM((chunks, lanes, width), bf16),
            pltpu.VMEM((cols, chunks, own, width), f32),
            pltpu.VMEM((rows, sources, own), f32),
            row_stat,
            row_stat,
            row_stat,
            col_stat,
            col_stat,
            col_stat,
            pltpu.VMEM((rows, chunks, width), f32),
            pltpu.VMEM((rows, rows, own), f32),
            pltpu.VMEM((rows, own, trades), bf16),
            piece,
            pltpu.VMEM((sources, trades), f32),
            *[piece] * 4,
            *[slim] * 2,
            dma((1,)),
            dma((cols - 1,)),
            dma((1,)),
            dma((4,)),
            *[dma((1,))] * 5,
            dma((PARTS * max(1, rows // 2 - 1),)),
            dma((rows // 2,)),
            dma((1,)),
            dma((CUTS * (cols // 2),)),
            dma((1,)),
            dma((PARTS * max(1, cols // 2 - 1),)),
            *[dma((1,))] * 3,
            dma((LAST,)),
            dma((11,)),
            pltpu.SemaphoreType.REGULAR((max(1, rows // 2 - 1),)),
        ],
        compiler_params=pltpu.CompilerParams(
            collective_id=0, has_side_effects=True, vmem_limit_bytes=LIMIT
        ),
    )(nodes_zero.T, nodes_one.T, nodes_two.T, precision[None, :], drift[None, :], terminal, ex1, ex0, flags)
    return handed(one, zero)


def hand(a, b, c, d, sems):
    copies = [pltpu.make_async_copy(a, c, sems.at[0]), pltpu.make_async_copy(b, d, sems.at[1])]
    for copy in copies:
        copy.start()
    for copy in copies:
        copy.wait()


def handed(one, zero):
    here = pl.BlockSpec(memory_space=pltpu.VMEM)
    out = jax.ShapeDtypeStruct(one.shape, one.dtype)
    return pl.pallas_call(
        hand,
        out_shape=(out, out),
        in_specs=[here, here],
        out_specs=(pl.BlockSpec(memory_space=pltpu.HBM),) * 2,
        scratch_shapes=[pltpu.SemaphoreType.DMA((2,))],
        compiler_params=pltpu.CompilerParams(vmem_limit_bytes=2 * 1024 * 1024),
    )(one, zero)


def solution(mesh):
    both = P(("row", "col"), None)
    return jax.shard_map(
        functools.partial(shards, mesh.shape["row"], mesh.shape["col"]),
        mesh=mesh,
        in_specs=(P("row", None), both, P("col", None), P(), P(), P("col", None), both, both, P()),
        out_specs=(both, both),
        check_vma=False,
    )
```

```python
import functools

import jax
import jax.numpy as jnp
from jax import lax
from jax.experimental import pallas as pl
from jax.experimental.pallas import tpu as pltpu
from jax.sharding import PartitionSpec as P

MESH = pl.DeviceIdType.MESH
TILE = 256
PARTS = 4
RELAY = 2
CUTS = 2
LAST = 2
LIMIT = 60 * 1024 * 1024


def flip(index, mask, size):
    bit = 1
    while bit < size:
        if mask & bit:
            index = index + bit - 2 * bit * lax.rem(lax.div(index, bit), 2)
        bit *= 2
    return index


def column_of(row):
    return jnp.broadcast_to(row, (128, row.shape[1])).T[:, :1]


def queries_of(nodes, precision, drift, height):
    shifted = nodes + drift
    offsets = 0.5 * jnp.sum(precision * shifted * shifted, axis=0, keepdims=True)
    first = offsets.astype(jnp.bfloat16).astype(jnp.float32)
    rest = offsets - first
    second = rest.astype(jnp.bfloat16).astype(jnp.float32)
    third = rest - second
    count = height - nodes.shape[0]
    at = lax.broadcasted_iota(jnp.int32, (count, nodes.shape[1]), 0)
    extra = jnp.where(at == 0, first, jnp.where(at == 1, second, jnp.where(at == 2, third, 0.0)))
    return jnp.concatenate([shifted * precision, extra], axis=0)


def upright(tall, lanes):
    short = lanes - tall.shape[0]
    if short:
        tall = jnp.concatenate([tall, jnp.zeros((short, tall.shape[1]), tall.dtype)], axis=0)
    return tall.T.astype(jnp.bfloat16)


def ones_under(count, width):
    at = lax.broadcasted_iota(jnp.int32, (count, width), 0)
    return jnp.where(at < 3, -1.0, 0.0).astype(jnp.bfloat16)


def settled(allowed, exercise, carried):
    return jnp.where(allowed == 1, jnp.maximum(exercise, carried), carried)


def scored(queries, targets):
    s = lax.dot_general(queries, targets, (((1,), (0,)), ((), ())), preferred_element_type=jnp.float32)
    fold = (s.shape[0] // 8, 8, s.shape[1])
    peak = jnp.max(jnp.max(s.reshape(fold), axis=0), axis=0, keepdims=True)
    x = jnp.exp(s - peak)
    return x, peak, jnp.sum(jnp.sum(x.reshape(fold), axis=0), axis=0, keepdims=True)


def merged(levels, totals):
    top = functools.reduce(jnp.maximum, levels)
    total = None
    for i, level in enumerate(levels):
        term = jnp.exp(level - top)
        if totals is not None:
            term = totals[i] * term
        total = term if total is None else total + term
    return top + jnp.log(total)


def body(
    rows,
    cols,
    nz_hbm,
    n1_hbm,
    n2_hbm,
    precision_hbm,
    drift_hbm,
    terminal_hbm,
    ex1_hbm,
    ex0_hbm,
    flags_hbm,
    v1_out,
    v0_out,
    precision_ref,
    drift_ref,
    flags_ref,
    nz_ref,
    n1_ref,
    n2_ref,
    terminal_ref,
    ex1_ref,
    ex0_ref,
    v1_ref,
    v0_ref,
    q1t,
    q1,
    t1,
    q0a,
    q0,
    t2,
    e1,
    e0,
    pk1,
    tt1,
    f1,
    pk0,
    tt0,
    f0,
    l1,
    l0p,
    l0,
    price,
    acc1,
    acc0,
    pair_out1,
    pair_in1,
    far_out1,
    far_in1,
    far_out0,
    far_in0,
    q_send,
    q_recv,
    t_send,
    t_recv,
    l1_send,
    l1_recv,
    l0p_send,
    l0p_recv,
    l0_send,
    l0_recv,
    p_send,
    p_recv,
    pc_recv,
    pair1_send,
    pair1_recv,
    far1_send,
    far1_recv,
    y_send,
    y_recv,
    far0_send,
    far0_recv,
    local,
    ready,
):
    r = lax.axis_index("row")
    c = lax.axis_index("col")
    depth, own = n1_ref.shape
    lanes = q0.shape[1]
    height = q1t.shape[1]
    _, chunks, _, width = e1.shape
    trades = price.shape[2]
    sources = q0.shape[0]
    blocks, _, _ = pk0.shape
    step = sources // blocks
    near = sources // 2
    group = 2 * lax.div(r, 2) + lax.rem(c, 2)

    def row_peer(m):
        return (flip(r, m, rows), c)

    def col_peer(s):
        return (r, flip(c, s, cols))

    def plane_peer(s):
        return (flip(r, s % 2, rows), flip(c, s - s % 2, cols))

    def remote(src, dst, send, recv, peer):
        return pltpu.make_async_remote_copy(
            src_ref=src, dst_ref=dst, send_sem=send, recv_sem=recv, device_id=peer, device_id_type=MESH
        )

    line = rows // 2
    deep = lax.div(r, 2)
    core = lax.rem(c, 2)
    beside = cols + jnp.where(deep > 0, 1, 0) + jnp.where(deep < line - 1, 1, 0)
    barrier = pltpu.get_barrier_semaphore()

    def call(sem):
        for s in range(1, cols):
            pl.semaphore_signal(sem, inc=1, device_id=col_peer(s), device_id_type=MESH)
        pl.semaphore_signal(sem, inc=1, device_id=row_peer(1), device_id_type=MESH)

        @pl.when(deep > 0)
        def _():
            pl.semaphore_signal(sem, inc=1, device_id=(r - 2, c), device_id_type=MESH)

        @pl.when(deep < line - 1)
        def _():
            pl.semaphore_signal(sem, inc=1, device_id=(r + 2, c), device_id_type=MESH)

    call(barrier)
    loads = [
        pltpu.make_async_copy(a, b, local.at[i])
        for i, (a, b) in enumerate(
            [
                (n1_hbm, n1_ref),
                (precision_hbm, precision_ref),
                (drift_hbm, drift_ref),
                (n2_hbm, n2_ref),
                (nz_hbm, nz_ref),
                (terminal_hbm, terminal_ref),
                (ex1_hbm, ex1_ref),
                (flags_hbm, flags_ref),
                (ex0_hbm, ex0_ref),
            ]
        )
    ]
    for load in loads:
        load.start()
    for load in loads[:3]:
        load.wait()
    precision = column_of(precision_ref[...])
    drift = column_of(drift_ref[...])
    mine = queries_of(n1_ref[...], precision, drift, height)
    q1t[0] = mine.astype(jnp.bfloat16)
    t1[0, :depth, :] = n1_ref[...].astype(jnp.bfloat16)
    pl.semaphore_wait(barrier, beside)
    call(ready.at[0])

    def q_copy(s, peer):
        return remote(q1t.at[0], q1t.at[s], q_send.at[0], q_recv.at[s - 1], peer)

    q_copy(1, col_peer(1)).start()
    for other in range(2):
        for s in range(2, cols, 2):
            slot = s + (1 - core if other else core)
            q_copy(slot, (r, flip(c, s, cols) - core + other)).start()

    def t_copy(m):
        if m % 2:
            src, peer = t1.at[m - 1, pl.ds(0, depth)], col_peer(1)
        else:
            src, peer = t1.at[0, pl.ds(0, depth)], row_peer(m)
        return remote(src, t1.at[m, pl.ds(0, depth)], t_send.at[0], t_recv.at[m % 2 + (2 if m >= 6 else 0)], peer)

    t_copy(1).start()
    if rows > 2:
        t_copy(2).start()

    q1[0] = upright(mine, lanes)
    for m in range(rows):
        t1[m, depth:, :] = ones_under(lanes - depth, own)
    loads[3].wait()
    for k in range(chunks):
        t2[k, :depth, :] = n2_ref[:, k * width : (k + 1) * width].astype(jnp.bfloat16)
        t2[k, depth:, :] = ones_under(lanes - depth, width)

    def stats_one(s):
        for k in range(chunks):
            x, peak, total = scored(q1[s], t2[k])
            e1[s, k] = x
            pk1[s, pl.ds(k, 1), :] = peak
            tt1[s, pl.ds(k, 1), :] = total

    def stats_zero(m, first, last):
        row = flip(group, m, rows)
        for b in range(first, last):
            x, peak, total = scored(q0[b * step : (b + 1) * step, :], t1[m])
            e0[m, b * step : (b + 1) * step, :] = x
            pk0[b, pl.ds(row, 1), :] = peak
            tt0[b, pl.ds(row, 1), :] = total

    def take_q(s):
        q_copy(s, col_peer(1)).wait_recv()
        q1[s] = upright(q1t[s].astype(jnp.float32), lanes)

    stats_one(0)
    loads[4].wait()
    q0a[...] = upright(queries_of(nz_ref[...], precision, drift, height), lanes)
    for s in range(0, cols, 2):
        at = pl.multiple_of(flip(c, s, cols) * own, own)
        q0[s // 2 * own : (s // 2 + 1) * own, :] = q0a[pl.ds(at, own), :]
    y_copy = remote(q0.at[pl.ds(0, near)], q0.at[pl.ds(near, near)], y_send.at[0], y_recv.at[0], row_peer(1))
    y_copy.start()
    rounds = ready.shape[0]

    def hear(i):
        pl.semaphore_wait(ready.at[i], beside)
        if i + 1 < rounds:
            call(ready.at[i + 1])

    take_q(1)
    hear(0)
    if rows > 4:
        t_copy(4).start()
    stats_one(1)
    stats_zero(0, 0, blocks // 2)
    for other in range(2):
        for s in range(2, cols, 2):
            slot = s + (core if other else 1 - core)
            take_q(slot)
            if other == 0 and s == 2:
                for i in range(1, rounds - 1):
                    hear(i)
                for m in range(6, rows, 2):
                    t_copy(m).start()
            stats_one(slot)

    def l1_copy(m):
        return remote(l1.at[0], l1.at[m], l1_send.at[0], l1_recv.at[0], row_peer(m))

    if rounds > 1:
        hear(rounds - 1)
    l1[0] = merged([pk1[s] for s in range(cols)], [tt1[s] for s in range(cols)])
    for m in reversed(range(1, rows)):
        l1_copy(m).start()

    def t_all(count, at):
        view = t1.at[pl.ds(0, count), pl.ds(0, depth)]
        return remote(view, view, t_send.at[0], t_recv.at[at], col_peer(1))

    first_ones, late_ones = range(2, min(6, rows), 2), range(6, rows, 2)
    if first_ones:
        t_all(len(first_ones), 0).wait_recv()
        for m in first_ones:
            t_copy(m + 1).start()
    y_copy.wait_recv()
    stats_zero(0, blocks // 2, blocks)
    for m in first_ones:
        stats_zero(m, 0, blocks)
    t_all(1 + len(first_ones), 1).wait_recv()
    if late_ones:
        t_all(len(late_ones), 2).wait_recv()
        for m in late_ones:
            t_copy(m + 1).start()
    for m in [1] + [m + 1 for m in first_ones]:
        stats_zero(m, 0, blocks)

    def weights_one(s, k, first, many):
        return (e1[s, k, first : first + many, :] * f1[s, k : k + 1, :]).astype(jnp.bfloat16)

    def partial_one(s, first, many):
        total = None
        for k in range(chunks):
            part = jnp.dot(
                weights_one(s, k, first, many), terminal_ref[k * width : (k + 1) * width, :], preferred_element_type=jnp.float32
            )
            total = part if total is None else total + part
        return total

    cut = own // CUTS

    def pair_copy(s, h):
        piece = pl.ds(h * cut, cut)
        at = h * (cols // 2) + s // 2
        return remote(
            pair_out1.at[s // 2, piece], pair_in1.at[s // 2, piece], pair1_send.at[0], pair1_recv.at[at], col_peer(1)
        )

    def far_copy(s, h):
        at = h * (cols // 2 - 1) + s // 2 - 1
        piece = pl.ds(h * size, size)
        return remote(
            far_out1.at[s // 2, piece], far_in1.at[s // 2, piece], far1_send.at[0], far1_recv.at[at], col_peer(s)
        )

    def last_copy(s, h):
        piece = pl.ds(h * count, count)
        return remote(far_out0.at[s, piece], far_in0.at[s, piece], far0_send.at[0], far0_recv.at[h], plane_peer(s))

    size = own // PARTS
    count = own // LAST
    away = list(range(2, cols, 2))

    l1_all = remote(l1.at[pl.ds(1, rows - 1)], l1.at[pl.ds(1, rows - 1)], l1_send.at[0], l1_recv.at[0], row_peer(1))
    l1_all.wait_recv()
    loads[5].wait()
    level = merged([l1[m] for m in range(rows)], None)
    for s in range(cols):
        f1[s] = jnp.exp(pk1[s] - level)
    def give_cut(s, h):
        pair_out1[s // 2, h * cut : (h + 1) * cut, :] = partial_one(s + 1, h * cut, cut)
        pair_copy(s, h).start()

    def give(s):
        for h in range(CUTS):
            give_cut(s, h)

    for s in away:
        give(s)
    for s in away:
        acc1[s // 2] = partial_one(s, 0, own)
    give_cut(0, 0)
    for h in range(CUTS):
        for s in away:
            pair_copy(s, h).wait_recv()
            for i in range(h * PARTS // CUTS, (h + 1) * PARTS // CUTS):
                piece = slice(i * size, (i + 1) * size)
                far_out1[s // 2, piece, :] = acc1[s // 2, piece, :] + pair_in1[s // 2, piece, :]
                far_copy(s, i).start()
    for h in range(1, CUTS):
        give_cut(0, h)
    for m in late_ones:
        stats_zero(m, 0, blocks)
    if late_ones:
        t_all(len(late_ones), 3).wait_recv()
    for m in late_ones:
        stats_zero(m + 1, 0, blocks)
    l0p[0] = merged([pk0[b] for b in range(blocks)], [tt0[b] for b in range(blocks)])
    l0_pair = remote(l0p.at[0], l0p.at[1], l0p_send.at[0], l0p_recv.at[0], col_peer(1))
    l0_pair.start()
    acc1[0] = partial_one(0, 0, own)
    for h in range(CUTS):
        pair_copy(0, h).wait_recv()
    held = acc1[0] + pair_in1[0]
    l0_pair.wait_recv()
    l0[0] = merged([l0p[0], l0p[1]], None)

    def l0_copy(m):
        return remote(l0.at[0], l0.at[m // 2], l0_send.at[0], l0_recv.at[0], row_peer(m))

    for m in reversed(range(2, rows, 2)):
        l0_copy(m).start()
    loads[6].wait()
    loads[7].wait()

    def p_copy(m, h):
        piece = pl.ds(h * size, size)
        if m % 2:
            src, peer, recv = price.at[m - 1, piece], col_peer(1), pc_recv.at[m // 2]
        else:
            recv = p_recv.at[h * (rows // 2 - 1) + m // 2 - 1]
            src, peer = (price.at[m - 2, piece], row_peer(2)) if relayed(m, h) else (price.at[0, piece], row_peer(m))
        return remote(src, price.at[m, piece], p_send.at[0], recv, peer)

    def relayed(m, h):
        return h < RELAY and m % 4 == 2 and m > 2

    def p_core(m):
        return remote(price.at[m], price.at[m], p_send.at[0], pc_recv.at[m // 2], col_peer(1))

    for h in range(PARTS):
        piece = slice(h * size, (h + 1) * size)
        carried = held[piece]
        for s in away:
            far_copy(s, h).wait_recv()
            carried = carried + far_in1[s // 2, piece, :]
        value = settled(flags_ref[1:2, :], ex1_ref[piece, :], carried)
        price[0, piece, :] = value.astype(jnp.bfloat16)
        for m in range(rows - 2, 0, -2):
            if not relayed(m, h):
                p_copy(m, h).start()
        p_copy(1, h).start()
        v1_ref[piece, :] = value
    keep_one = pltpu.make_async_copy(v1_ref, v1_out, local.at[9])
    keep_one.start()
    def add_zero(m, row, first, count):
        parts = []
        each = min(step, count)
        for at in range(first, first + count, each):
            w = (e0[m, at : at + each, :] * f0[at // step, pl.ds(row, 1), :]).astype(jnp.bfloat16)
            parts.append(jnp.dot(w, price[m], preferred_element_type=jnp.float32))
        return parts[0] if len(parts) == 1 else jnp.concatenate(parts, axis=0)

    def gain(slots):
        for at in range(0, sources, step):
            total = acc0[at : at + step, :] if 0 not in slots else None
            for m in slots:
                part = add_zero(m, flip(group, m, rows), at, step)
                total = part if total is None else total + part
            acc0[at : at + step, :] = total

    def pass_on(m, h):
        p_copy(m, h).wait_recv()
        if m + 2 < rows and relayed(m + 2, h) and m % 4 == 0:
            p_copy(m + 2, h).start()
        p_copy(m + 1, h).start()

    def l0_all():
        view = l0.at[pl.ds(1, rows // 2 - 1)]
        return remote(view, view, l0_send.at[0], l0_recv.at[0], row_peer(1))

    def ready_zero():
        if rows > 2:
            l0_all().wait_recv()
        level = merged([l0[i] for i in range(rows // 2)], None)
        for b in range(blocks):
            f0[b] = jnp.exp(pk0[b] - level)

    direct = [m for m in range(2, rows, 2) if m % 4 == 0 or m == 2]
    other = [m for m in range(2, rows, 2) if m not in direct]
    for h in range(PARTS):
        for m in reversed(direct):
            pass_on(m, h)
        for m in other:
            if not relayed(m, h):
                pass_on(m, h)
        if h == PARTS // 2 - 1:
            ready_zero()
            p_core(1).wait_recv()
            gain([0, 1])
    gain(direct)
    for h in range(min(RELAY, PARTS)):
        for m in other:
            pass_on(m, h)
    ahead = [m for m in range(3, rows - 2, 2)]
    for m in ahead:
        p_core(m).wait_recv()
    if ahead:
        gain(ahead)

    @pl.when(core == 0)
    def _():
        if rows > 2:
            p_core(rows - 1).wait_recv()
        if other:
            gain(other[:-1] + [rows - 1])

    @pl.when(core == 1)
    def _():
        if other:
            gain(other)
        if rows > 2:
            p_core(rows - 1).wait_recv()

    if other:
        final, final_row = rows - 2 + core, flip(group, rows - 2, rows) - core
    else:
        final, final_row = rows - 1, flip(group, rows - 1, rows)
    held = None
    for s in [s + 1 for s in away] + away + [1, 0]:
        at = (s % 2) * near + s // 2 * own
        total = acc0[at : at + own, :] + add_zero(final, final_row, at, own)
        if s:
            far_out0[s] = total.astype(far_out0.dtype)
            for h in range(LAST):
                last_copy(s, h).start()
        else:
            held = total
    loads[8].wait()
    for h in range(LAST):
        piece = slice(h * count, (h + 1) * count)
        carried = held[piece]
        view = far_in0.at[pl.ds(1, cols - 1), pl.ds(h * count, count)]
        remote(view, view, far0_send.at[0], far0_recv.at[h], col_peer(1)).wait_recv()
        for s in range(1, cols):
            carried = carried + far_in0[s, piece, :].astype(jnp.float32)
        v0_ref[piece, :] = settled(flags_ref[0:1, :], ex0_ref[piece, :], carried)
    keep_zero = pltpu.make_async_copy(v0_ref, v0_out, local.at[10])
    keep_zero.start()

    y_copy.wait_send()

    def sent(ref, first, count, sem):
        view = ref.at[pl.ds(first, count)]
        remote(view, view, sem.at[0], y_recv.at[0], col_peer(1)).wait_send()

    sent(q1t, 0, cols - 1, q_send)
    t_all(rows - 1, 0).wait_send()
    l1_all.wait_send()
    l0_pair.wait_send()
    if rows > 2:
        l0_all().wait_send()
    sent(price, 0, rows - 1, p_send)
    sent(pair_out1, 0, cols // 2, pair1_send)
    if away:
        sent(far_out1, 1, cols // 2 - 1, far1_send)
    sent(far_out0, 1, cols - 1, far0_send)
    keep_one.wait()
    keep_zero.wait()


def shards(rows, cols, nodes_zero, nodes_one, nodes_two, precision, drift, terminal, ex1, ex0, flags):
    own, depth = nodes_one.shape
    height = depth + 16
    sources = nodes_zero.shape[0]
    targets = nodes_two.shape[0]
    trades = terminal.shape[1]
    width = min(TILE, targets)
    chunks = targets // width
    step = max(own, min(TILE, sources))
    blocks = sources // step
    lanes = 128 * (-(-(depth + 3) // 128))
    dma = pltpu.SemaphoreType.DMA
    f32, bf16 = jnp.float32, jnp.bfloat16
    row_stat = pltpu.VMEM((cols, chunks, width), f32)
    col_stat = pltpu.VMEM((blocks, rows, own), f32)
    piece = pltpu.VMEM((cols // 2, own, trades), f32)
    slim = pltpu.VMEM((cols, own, trades), bf16)
    mine = pltpu.VMEM((own, trades), f32)
    one, zero = pl.pallas_call(
        functools.partial(body, rows, cols),
        out_shape=(pltpu.VMEM((own, trades), f32),) * 2,
        in_specs=[pl.BlockSpec(memory_space=pltpu.HBM)] * 9,
        out_specs=(pl.BlockSpec(memory_space=pl.ANY),) * 2,
        scratch_shapes=[
            pltpu.VMEM((1, depth), f32),
            pltpu.VMEM((1, depth), f32),
            pltpu.VMEM((2, trades), jnp.int32),
            pltpu.VMEM((depth, sources), f32),
            pltpu.VMEM((depth, own), f32),
            pltpu.VMEM((depth, targets), f32),
            pltpu.VMEM((targets, trades), bf16),
            *[mine] * 4,
            pltpu.VMEM((cols, height, own), bf16),
            pltpu.VMEM((cols, own, lanes), bf16),
            pltpu.VMEM((rows, lanes, own), bf16),
            pltpu.VMEM((sources, lanes), bf16),
            pltpu.VMEM((sources, lanes), bf16),
            pltpu.VMEM((chunks, lanes, width), bf16),
            pltpu.VMEM((cols, chunks, own, width), f32),
            pltpu.VMEM((rows, sources, own), f32),
            row_stat,
            row_stat,
            row_stat,
            col_stat,
            col_stat,
            col_stat,
            pltpu.VMEM((rows, chunks, width), f32),
            pltpu.VMEM((2, rows, own), f32),
            pltpu.VMEM((rows // 2, rows, own), f32),
            pltpu.VMEM((rows, own, trades), bf16),
            piece,
            pltpu.VMEM((sources, trades), f32),
            *[piece] * 4,
            *[slim] * 2,
            dma((1,)),
            dma((cols - 1,)),
            dma((1,)),
            dma((4,)),
            *[dma((1,))] * 7,
            dma((PARTS * max(1, rows // 2 - 1),)),
            dma((rows // 2,)),
            dma((1,)),
            dma((CUTS * (cols // 2),)),
            dma((1,)),
            dma((PARTS * max(1, cols // 2 - 1),)),
            *[dma((1,))] * 3,
            dma((LAST,)),
            dma((11,)),
            pltpu.SemaphoreType.REGULAR((max(1, rows // 2 - 1),)),
        ],
        compiler_params=pltpu.CompilerParams(
            collective_id=0, has_side_effects=True, vmem_limit_bytes=LIMIT
        ),
    )(nodes_zero.T, nodes_one.T, nodes_two.T, precision[None, :], drift[None, :], terminal, ex1, ex0, flags)
    return handed(one, zero)


def hand(a, b, c, d, sems):
    copies = [pltpu.make_async_copy(a, c, sems.at[0]), pltpu.make_async_copy(b, d, sems.at[1])]
    for copy in copies:
        copy.start()
    for copy in copies:
        copy.wait()


def handed(one, zero):
    here = pl.BlockSpec(memory_space=pltpu.VMEM)
    out = jax.ShapeDtypeStruct(one.shape, one.dtype)
    return pl.pallas_call(
        hand,
        out_shape=(out, out),
        in_specs=[here, here],
        out_specs=(pl.BlockSpec(memory_space=pltpu.HBM),) * 2,
        scratch_shapes=[pltpu.SemaphoreType.DMA((2,))],
        compiler_params=pltpu.CompilerParams(vmem_limit_bytes=2 * 1024 * 1024),
    )(one, zero)


def solution(mesh):
    both = P(("row", "col"), None)
    return jax.shard_map(
        functools.partial(shards, mesh.shape["row"], mesh.shape["col"]),
        mesh=mesh,
        in_specs=(P("row", None), both, P("col", None), P(), P(), P("col", None), both, both, P()),
        out_specs=(both, both),
        check_vma=False,
    )
```

```python
import functools

import jax
import jax.numpy as jnp
from jax import lax
from jax.experimental import pallas as pl
from jax.experimental.pallas import tpu as pltpu
from jax.sharding import PartitionSpec as P

MESH = pl.DeviceIdType.MESH
TILE = 256
PARTS = 4
RELAY = 1
CUTS = 2
LAST = 2
LIMIT = 60 * 1024 * 1024


def flip(index, mask, size):
    bit = 1
    while bit < size:
        if mask & bit:
            index = index + bit - 2 * bit * lax.rem(lax.div(index, bit), 2)
        bit *= 2
    return index


def column_of(row):
    return jnp.broadcast_to(row, (128, row.shape[1])).T[:, :1]


def queries_of(nodes, precision, drift, height):
    shifted = nodes + drift
    offsets = 0.5 * jnp.sum(precision * shifted * shifted, axis=0, keepdims=True)
    first = offsets.astype(jnp.bfloat16).astype(jnp.float32)
    rest = offsets - first
    second = rest.astype(jnp.bfloat16).astype(jnp.float32)
    third = rest - second
    count = height - nodes.shape[0]
    at = lax.broadcasted_iota(jnp.int32, (count, nodes.shape[1]), 0)
    extra = jnp.where(at == 0, first, jnp.where(at == 1, second, jnp.where(at == 2, third, 0.0)))
    return jnp.concatenate([shifted * precision, extra], axis=0)


def upright(tall, lanes):
    short = lanes - tall.shape[0]
    if short:
        tall = jnp.concatenate([tall, jnp.zeros((short, tall.shape[1]), tall.dtype)], axis=0)
    return tall.T.astype(jnp.bfloat16)


def ones_under(count, width):
    at = lax.broadcasted_iota(jnp.int32, (count, width), 0)
    return jnp.where(at < 3, -1.0, 0.0).astype(jnp.bfloat16)


def turned(x):
    mid = x.shape[1] // 2
    return jnp.concatenate([x[:, mid:], x[:, :mid]], axis=1)


def mixed(a, b):
    low = lax.broadcasted_iota(jnp.int32, a.shape, 1) < a.shape[1] // 2
    return jnp.where(low, a, b)


def packed(x):
    top, bottom = x[: x.shape[0] // 2], turned(x[x.shape[0] // 2 :])
    return jnp.concatenate([mixed(top, bottom), mixed(bottom, top)], axis=0)


def unpacked(x):
    a, b = x[: x.shape[0] // 2], x[x.shape[0] // 2 :]
    return jnp.concatenate([mixed(a, b), turned(mixed(b, a))], axis=0)


def floor_of(allowed, exercise):
    return packed(jnp.where(allowed == 1, exercise, -jnp.inf))


def scored(queries, targets):
    s = lax.dot_general(queries, targets, (((1,), (0,)), ((), ())), preferred_element_type=jnp.float32)
    fold = (s.shape[0] // 8, 8, s.shape[1])
    peak = jnp.max(jnp.max(s.reshape(fold), axis=0), axis=0, keepdims=True)
    x = jnp.exp(s - peak)
    return x, peak, jnp.sum(jnp.sum(x.reshape(fold), axis=0), axis=0, keepdims=True)


def merged(levels, totals):
    top = functools.reduce(jnp.maximum, levels)
    total = None
    for i, level in enumerate(levels):
        term = jnp.exp(level - top)
        if totals is not None:
            term = totals[i] * term
        total = term if total is None else total + term
    return top + jnp.log(total)


def body(
    rows,
    cols,
    nz_hbm,
    n1_hbm,
    n2_hbm,
    precision_hbm,
    drift_hbm,
    terminal_hbm,
    ex1_hbm,
    ex0_hbm,
    flags_hbm,
    v1_out,
    v0_out,
    precision_ref,
    drift_ref,
    flags_ref,
    nz_ref,
    n1_ref,
    n2_ref,
    terminal_ref,
    ex1_ref,
    ex0_ref,
    v1_ref,
    v0_ref,
    q1t,
    q1,
    t1,
    q0a,
    q0,
    wz,
    t2,
    e1,
    e0,
    pk1,
    tt1,
    f1,
    pk0,
    tt0,
    f0,
    l1,
    l0p,
    l0,
    price,
    acc1,
    acc0,
    pair_out1,
    pair_in1,
    far_out1,
    far_in1,
    far_out0,
    far_in0,
    q_send,
    q_recv,
    t_send,
    t_recv,
    l1_send,
    l1_recv,
    l0p_send,
    l0p_recv,
    l0_send,
    l0_recv,
    p_send,
    p_recv,
    pc_recv,
    pair1_send,
    pair1_recv,
    far1_send,
    far1_recv,
    y_send,
    y_recv,
    far0_send,
    far0_recv,
    local,
    ready,
):
    r = lax.axis_index("row")
    c = lax.axis_index("col")
    depth, own = n1_ref.shape
    lanes = q0a.shape[1]
    height = q1t.shape[1]
    _, chunks, _, width = e1.shape
    trades = price.shape[2]
    sources = q0a.shape[0]
    blocks, _, _ = pk0.shape
    step = sources // blocks
    half_own = own // 2
    near = sources // 2
    quarter = sources // 4
    group = 2 * lax.div(r, 2) + lax.rem(c, 2)

    def row_peer(m):
        return (flip(r, m, rows), c)

    def col_peer(s):
        return (r, flip(c, s, cols))

    def plane_peer(s):
        return (flip(r, s % 2, rows), flip(c, s - s % 2, cols))

    def remote(src, dst, send, recv, peer):
        return pltpu.make_async_remote_copy(
            src_ref=src, dst_ref=dst, send_sem=send, recv_sem=recv, device_id=peer, device_id_type=MESH
        )

    line = rows // 2
    deep = lax.div(r, 2)
    core = lax.rem(c, 2)
    beside = cols + jnp.where(deep > 0, 1, 0) + jnp.where(deep < line - 1, 1, 0)
    barrier = pltpu.get_barrier_semaphore()

    def call(sem):
        for s in range(1, cols):
            pl.semaphore_signal(sem, inc=1, device_id=col_peer(s), device_id_type=MESH)
        pl.semaphore_signal(sem, inc=1, device_id=row_peer(1), device_id_type=MESH)

        @pl.when(deep > 0)
        def _():
            pl.semaphore_signal(sem, inc=1, device_id=(r - 2, c), device_id_type=MESH)

        @pl.when(deep < line - 1)
        def _():
            pl.semaphore_signal(sem, inc=1, device_id=(r + 2, c), device_id_type=MESH)

    call(barrier)
    loads = [
        pltpu.make_async_copy(a, b, local.at[i])
        for i, (a, b) in enumerate(
            [
                (n1_hbm, n1_ref),
                (precision_hbm, precision_ref),
                (drift_hbm, drift_ref),
                (n2_hbm, n2_ref),
                (nz_hbm, nz_ref),
                (terminal_hbm, terminal_ref),
                (ex1_hbm, ex1_ref),
                (flags_hbm, flags_ref),
                (ex0_hbm, ex0_ref),
            ]
        )
    ]
    for load in loads:
        load.start()
    for load in loads[:3]:
        load.wait()
    precision = column_of(precision_ref[...])
    drift = column_of(drift_ref[...])
    mine = queries_of(n1_ref[...], precision, drift, height)
    q1t[0] = mine.astype(jnp.bfloat16)
    t1[0, :depth, :] = n1_ref[...].astype(jnp.bfloat16)
    pl.semaphore_wait(barrier, beside)
    call(ready.at[0])

    def q_copy(s, peer):
        return remote(q1t.at[0], q1t.at[s], q_send.at[0], q_recv.at[s - 1], peer)

    q_copy(1, col_peer(1)).start()
    for other in range(2):
        for s in range(2, cols, 2):
            slot = s + (1 - core if other else core)
            q_copy(slot, (r, flip(c, s, cols) - core + other)).start()

    def t_copy(m):
        if m % 2:
            src, peer = t1.at[m - 1, pl.ds(0, depth)], col_peer(1)
        else:
            src, peer = t1.at[0, pl.ds(0, depth)], row_peer(m)
        return remote(src, t1.at[m, pl.ds(0, depth)], t_send.at[0], t_recv.at[m % 2 + (2 if m >= 6 else 0)], peer)

    t_copy(1).start()
    if rows > 2:
        t_copy(2).start()

    q1[0] = upright(mine, lanes)
    for m in range(rows):
        t1[m, depth:, :] = ones_under(lanes - depth, own)
    loads[3].wait()
    for k in range(chunks):
        t2[k, :depth, :] = n2_ref[:, k * width : (k + 1) * width].astype(jnp.bfloat16)
        t2[k, depth:, :] = ones_under(lanes - depth, width)

    def stats_one(s):
        for k in range(chunks):
            x, peak, total = scored(q1[s], t2[k])
            e1[s, k] = x
            pk1[s, pl.ds(k, 1), :] = peak
            tt1[s, pl.ds(k, 1), :] = total

    every = (0, 1, 2, 3)

    def stats_zero(m, which):
        row = flip(group, m, rows)
        for b in which:
            x, peak, total = scored(q0[b // 2, b % 2], t1[m])
            e0[m, b * step : (b + 1) * step, :] = x
            pk0[b, pl.ds(row, 1), :] = peak
            tt0[b, pl.ds(row, 1), :] = total

    def take_q(s):
        q_copy(s, col_peer(1)).wait_recv()
        q1[s] = upright(q1t[s].astype(jnp.float32), lanes)

    stats_one(0)
    loads[4].wait()
    q0a[...] = upright(queries_of(nz_ref[...], precision, drift, height), lanes)
    for s in range(0, cols, 2):
        at = pl.multiple_of(flip(c, s, cols) * own, own)
        for side in range(2):
            q0[side, 0, s // 2 * half_own : (s // 2 + 1) * half_own, :] = q0a[pl.ds(at + side * half_own, half_own), :]
    y_copy = remote(q0.at[:, 0], q0.at[:, 1], y_send.at[0], y_recv.at[0], row_peer(1))
    y_copy.start()
    rounds = ready.shape[0]

    def hear(i):
        pl.semaphore_wait(ready.at[i], beside)
        if i + 1 < rounds:
            call(ready.at[i + 1])

    take_q(1)
    hear(0)
    if rows > 4:
        t_copy(4).start()
    stats_one(1)
    stats_zero(0, (0, 2))
    for other in range(2):
        for s in range(2, cols, 2):
            slot = s + (core if other else 1 - core)
            take_q(slot)
            if other == 0 and s == 2:
                for i in range(1, rounds - 1):
                    hear(i)
                for m in range(6, rows, 2):
                    t_copy(m).start()
            stats_one(slot)

    def l1_copy(m):
        return remote(l1.at[0], l1.at[m], l1_send.at[0], l1_recv.at[0], row_peer(m))

    if rounds > 1:
        hear(rounds - 1)
    l1[0] = merged([pk1[s] for s in range(cols)], [tt1[s] for s in range(cols)])
    for m in reversed(range(1, rows)):
        l1_copy(m).start()

    def t_all(count, at):
        view = t1.at[pl.ds(0, count), pl.ds(0, depth)]
        return remote(view, view, t_send.at[0], t_recv.at[at], col_peer(1))

    first_ones, late_ones = range(2, min(6, rows), 2), range(6, rows, 2)
    if first_ones:
        t_all(len(first_ones), 0).wait_recv()
        for m in first_ones:
            t_copy(m + 1).start()
    y_copy.wait_recv()
    stats_zero(0, (1, 3))
    for m in first_ones:
        stats_zero(m, every)
    t_all(1 + len(first_ones), 1).wait_recv()
    if late_ones:
        t_all(len(late_ones), 2).wait_recv()
        for m in late_ones:
            t_copy(m + 1).start()
    for m in [1] + [m + 1 for m in first_ones]:
        stats_zero(m, every)

    def weights_one(s, k):
        return (e1[s, k] * f1[s, k : k + 1, :]).astype(jnp.bfloat16)

    def partial_one(s):
        total = None
        for k in range(chunks):
            part = jnp.dot(
                weights_one(s, k), terminal_ref[k * width : (k + 1) * width, :], preferred_element_type=jnp.float32
            )
            total = part if total is None else total + part
        return packed(total)

    cut = own // CUTS

    def pair_copy(s, h):
        piece = pl.ds(h * cut, cut)
        at = h * (cols // 2) + s // 2
        return remote(
            pair_out1.at[s // 2, piece], pair_in1.at[s // 2, piece], pair1_send.at[0], pair1_recv.at[at], col_peer(1)
        )

    def far_copy(s, h):
        at = h * (cols // 2 - 1) + s // 2 - 1
        piece = pl.ds(h * size, size)
        return remote(
            far_out1.at[s // 2, piece], far_in1.at[s // 2, piece], far1_send.at[0], far1_recv.at[at], col_peer(s)
        )

    def last_copy(s, h):
        piece = pl.ds(h * count, count)
        return remote(far_out0.at[s, piece], far_in0.at[s, piece], far0_send.at[0], far0_recv.at[h], plane_peer(s))

    size = own // PARTS
    count = own // LAST
    away = list(range(2, cols, 2))

    l1_all = remote(l1.at[pl.ds(1, rows - 1)], l1.at[pl.ds(1, rows - 1)], l1_send.at[0], l1_recv.at[0], row_peer(1))
    l1_all.wait_recv()
    loads[5].wait()
    level = merged([l1[m] for m in range(rows)], None)
    for s in range(cols):
        f1[s] = jnp.exp(pk1[s] - level)

    def give(s):
        total = partial_one(s + 1)
        for h in range(CUTS):
            pair_out1[s // 2, h * cut : (h + 1) * cut, :] = total[h * cut : (h + 1) * cut]
            pair_copy(s, h).start()

    for s in away:
        give(s)
    for s in away:
        acc1[s // 2] = partial_one(s)
    give(0)
    for h in range(CUTS):
        for s in away:
            pair_copy(s, h).wait_recv()
            for i in range(h * PARTS // CUTS, (h + 1) * PARTS // CUTS):
                piece = slice(i * size, (i + 1) * size)
                far_out1[s // 2, piece, :] = acc1[s // 2, piece, :] + pair_in1[s // 2, piece, :]
                far_copy(s, i).start()
    for m in late_ones:
        stats_zero(m, every)
    if late_ones:
        t_all(len(late_ones), 3).wait_recv()
    for m in late_ones:
        stats_zero(m + 1, every)
    l0p[0] = merged([pk0[b] for b in range(blocks)], [tt0[b] for b in range(blocks)])
    l0_pair = remote(l0p.at[0], l0p.at[1], l0p_send.at[0], l0p_recv.at[0], col_peer(1))
    l0_pair.start()
    acc1[0] = partial_one(0)
    for load in loads[6:]:
        load.wait()
    ex1_ref[...] = floor_of(flags_ref[1:2, :], ex1_ref[...])
    ex0_ref[...] = floor_of(flags_ref[0:1, :], ex0_ref[...])
    for h in range(CUTS):
        pair_copy(0, h).wait_recv()
    held = acc1[0] + pair_in1[0]
    l0_pair.wait_recv()
    l0[0] = merged([l0p[0], l0p[1]], None)

    def l0_copy(m):
        return remote(l0.at[0], l0.at[m // 2], l0_send.at[0], l0_recv.at[0], row_peer(m))

    for m in reversed(range(2, rows, 2)):
        l0_copy(m).start()

    def p_copy(m, h):
        piece = pl.ds(h * size, size)
        if m % 2:
            src, peer, recv = price.at[m - 1, piece], col_peer(1), pc_recv.at[h * 2 // PARTS * line + m // 2]
        else:
            recv = p_recv.at[h * (rows // 2 - 1) + m // 2 - 1]
            src, peer = (price.at[m - 2, piece], row_peer(2)) if relayed(m, h) else (price.at[0, piece], row_peer(m))
        return remote(src, price.at[m, piece], p_send.at[0], recv, peer)

    def relayed(m, h):
        return h < RELAY and m % 4 == 2 and m > 2

    def p_core(m, half):
        view = price.at[m, pl.ds(half * half_own, half_own)]
        return remote(view, view, p_send.at[0], pc_recv.at[half * line + m // 2], col_peer(1))

    for h in range(PARTS):
        piece = slice(h * size, (h + 1) * size)
        carried = held[piece]
        for s in away:
            far_copy(s, h).wait_recv()
            carried = carried + far_in1[s // 2, piece, :]
        value = jnp.maximum(ex1_ref[piece, :], carried)
        price[0, piece, :] = value.astype(jnp.bfloat16)
        for m in range(rows - 2, 0, -2):
            if not relayed(m, h):
                p_copy(m, h).start()
        p_copy(1, h).start()
        v1_ref[piece, :] = value
    def weigh(m):
        row = flip(group, m, rows)
        for b in range(blocks):
            part = e0[m, b * step : (b + 1) * step, :] * f0[b, pl.ds(row, 1), :]
            wz[m, b * step : (b + 1) * step, :] = part.astype(jnp.bfloat16)

    def sides(m, half):
        p = price[m, half * half_own : (half + 1) * half_own, :].astype(jnp.float32)
        t = turned(p)
        return p, t

    def stacked(a, b):
        return jnp.concatenate([a, b], axis=0).astype(jnp.bfloat16)

    def times(m, first, many, right):
        return jnp.dot(wz[m, pl.ds(first, many), :], right, preferred_element_type=jnp.float32)

    def rights(m, half):
        p = price[m, half * half_own : (half + 1) * half_own, :]
        t = turned(p)
        return m, jnp.concatenate([p, t], axis=0), jnp.concatenate([t, p], axis=0)

    def products(pairs, at):
        upper = lower = None
        for m, right, left in pairs:
            a = times(m, at, quarter, right)
            b = times(m, near + at, quarter, left)
            upper = a if upper is None else upper + a
            lower = b if lower is None else lower + b
        return upper, lower

    def gain_both(slots):
        pairs = []
        for m in slots:
            weigh(m)
            (pa, ta), (pb, tb) = sides(m, 0), sides(m, 1)
            pairs.append((m, stacked(mixed(pa, pb), mixed(ta, tb)), stacked(mixed(tb, ta), mixed(pb, pa))))
        for at in range(0, near, quarter):
            upper, lower = products(pairs, at)
            acc0[0, at : at + quarter, :] = mixed(upper, lower)
            acc0[1, at : at + quarter, :] = mixed(lower, upper)

    def product(pairs, half, at):
        upper, lower = products(pairs, at)
        return mixed(lower, upper) if half else mixed(upper, lower)

    def gain(slots, half):
        pairs = [rights(m, half) for m in slots]
        for at in range(0, near, quarter):
            acc0[half, at : at + quarter, :] = acc0[half, at : at + quarter, :] + product(pairs, half, at)

    def pass_on(m, h):
        p_copy(m, h).wait_recv()
        if m + 2 < rows and relayed(m + 2, h) and m % 4 == 0:
            p_copy(m + 2, h).start()
        p_copy(m + 1, h).start()

    def l0_all():
        view = l0.at[pl.ds(1, rows // 2 - 1)]
        return remote(view, view, l0_send.at[0], l0_recv.at[0], row_peer(1))

    def ready_zero():
        if rows > 2:
            l0_all().wait_recv()
        level = merged([l0[i] for i in range(rows // 2)], None)
        for b in range(blocks):
            f0[b] = jnp.exp(pk0[b] - level)

    direct = [m for m in range(2, rows, 2) if m % 4 == 0 or m == 2]
    other = [m for m in range(2, rows, 2) if m not in direct]
    ahead = [m for m in range(3, rows - 2, 2)]

    def pass_all(h):
        for m in reversed(direct):
            pass_on(m, h)
        for m in other:
            if not relayed(m, h):
                pass_on(m, h)

    def finish(half):
        pairs = [rights(final, half)]
        here = slice(half * half_own, (half + 1) * half_own)
        for dy in (1, 0):
            total = acc0[half, dy * quarter : (dy + 1) * quarter, :] + product(pairs, half, dy * quarter)
            for s in [s + dy for s in away] + [dy]:
                part = total[s // 2 * half_own : (s // 2 + 1) * half_own]
                if s:
                    far_out0[s, here, :] = part.astype(far_out0.dtype)
                    last_copy(s, half).start()
                else:
                    v0_ref[here, :] = part

    def mid_core(half, early):
        for m in ahead:
            p_core(m, half).wait_recv()

        @pl.when(core == 0)
        def _():
            if rows > 2:
                p_core(rows - 1, half).wait_recv()
            slots = early + ahead + (other[:-1] + [rows - 1] if other else [])
            if slots:
                gain(slots, half)

        @pl.when(core == 1)
        def _():
            slots = early + ahead + other
            if slots:
                gain(slots, half)
            if rows > 2:
                p_core(rows - 1, half).wait_recv()

    final = rows - 2 + core if other else rows - 1
    pass_all(0)
    ready_zero()
    for half in range(2):
        p_core(1, half).wait_recv()
    gain_both([0, 1])
    for m in range(2, rows):
        weigh(m)
    v1_ref[...] = unpacked(v1_ref[...])
    keep_one = pltpu.make_async_copy(v1_ref, v1_out, local.at[9])
    keep_one.start()
    for h in range(1, PARTS // 2):
        pass_all(h)
    gain(direct, 0)
    for h in range(min(RELAY, PARTS // 2)):
        for m in other:
            pass_on(m, h)
    pass_all(PARTS // 2)
    mid_core(0, [])
    for h in range(PARTS // 2 + 1, PARTS):
        pass_all(h)
    finish(0)
    gain(direct, 1)
    mid_core(1, [])
    finish(1)
    for h in range(LAST):
        piece = slice(h * count, (h + 1) * count)
        view = far_in0.at[pl.ds(1, cols - 1), pl.ds(h * count, count)]
        remote(view, view, far0_send.at[0], far0_recv.at[h], col_peer(1)).wait_recv()
        carried = v0_ref[piece, :]
        for s in range(1, cols):
            carried = carried + far_in0[s, piece, :].astype(jnp.float32)
        v0_ref[piece, :] = jnp.maximum(ex0_ref[piece, :], carried)
    v0_ref[...] = unpacked(v0_ref[...])
    keep_zero = pltpu.make_async_copy(v0_ref, v0_out, local.at[10])
    keep_zero.start()

    y_copy.wait_send()

    def sent(ref, first, count, sem):
        view = ref.at[pl.ds(first, count)]
        remote(view, view, sem.at[0], y_recv.at[0], col_peer(1)).wait_send()

    sent(q1t, 0, cols - 1, q_send)
    t_all(rows - 1, 0).wait_send()
    l1_all.wait_send()
    l0_pair.wait_send()
    if rows > 2:
        l0_all().wait_send()
    sent(price, 0, rows - 1, p_send)
    sent(pair_out1, 0, cols // 2, pair1_send)
    if away:
        sent(far_out1, 1, cols // 2 - 1, far1_send)
    sent(far_out0, 1, cols - 1, far0_send)
    keep_one.wait()
    keep_zero.wait()


def shards(rows, cols, nodes_zero, nodes_one, nodes_two, precision, drift, terminal, ex1, ex0, flags):
    own, depth = nodes_one.shape
    height = depth + 16
    sources = nodes_zero.shape[0]
    targets = nodes_two.shape[0]
    trades = terminal.shape[1]
    width = min(TILE, targets)
    chunks = targets // width
    blocks = 4
    lanes = 128 * (-(-(depth + 3) // 128))
    dma = pltpu.SemaphoreType.DMA
    f32, bf16 = jnp.float32, jnp.bfloat16
    row_stat = pltpu.VMEM((cols, chunks, width), f32)
    col_stat = pltpu.VMEM((blocks, rows, own), f32)
    piece = pltpu.VMEM((cols // 2, own, trades), f32)
    slim = pltpu.VMEM((cols, own, trades), bf16)
    mine = pltpu.VMEM((own, trades), f32)
    one, zero = pl.pallas_call(
        functools.partial(body, rows, cols),
        out_shape=(pltpu.VMEM((own, trades), f32),) * 2,
        in_specs=[pl.BlockSpec(memory_space=pltpu.HBM)] * 9,
        out_specs=(pl.BlockSpec(memory_space=pl.ANY),) * 2,
        scratch_shapes=[
            pltpu.VMEM((1, depth), f32),
            pltpu.VMEM((1, depth), f32),
            pltpu.VMEM((2, trades), jnp.int32),
            pltpu.VMEM((depth, sources), f32),
            pltpu.VMEM((depth, own), f32),
            pltpu.VMEM((depth, targets), f32),
            pltpu.VMEM((targets, trades), bf16),
            *[mine] * 4,
            pltpu.VMEM((cols, height, own), bf16),
            pltpu.VMEM((cols, own, lanes), bf16),
            pltpu.VMEM((rows, lanes, own), bf16),
            pltpu.VMEM((sources, lanes), bf16),
            pltpu.VMEM((2, 2, sources // 4, lanes), bf16),
            pltpu.VMEM((rows, sources, own), bf16),
            pltpu.VMEM((chunks, lanes, width), bf16),
            pltpu.VMEM((cols, chunks, own, width), f32),
            pltpu.VMEM((rows, sources, own), f32),
            row_stat,
            row_stat,
            row_stat,
            col_stat,
            col_stat,
            col_stat,
            pltpu.VMEM((rows, chunks, width), f32),
            pltpu.VMEM((2, rows, own), f32),
            pltpu.VMEM((rows // 2, rows, own), f32),
            pltpu.VMEM((rows, own, trades), bf16),
            piece,
            pltpu.VMEM((2, sources // 2, trades), f32),
            *[piece] * 4,
            *[slim] * 2,
            dma((1,)),
            dma((cols - 1,)),
            dma((1,)),
            dma((4,)),
            *[dma((1,))] * 7,
            dma((PARTS * max(1, rows // 2 - 1),)),
            dma((rows,)),
            dma((1,)),
            dma((CUTS * (cols // 2),)),
            dma((1,)),
            dma((PARTS * max(1, cols // 2 - 1),)),
            *[dma((1,))] * 3,
            dma((LAST,)),
            dma((11,)),
            pltpu.SemaphoreType.REGULAR((max(1, rows // 2 - 1),)),
        ],
        compiler_params=pltpu.CompilerParams(
            collective_id=0, has_side_effects=True, vmem_limit_bytes=LIMIT
        ),
    )(nodes_zero.T, nodes_one.T, nodes_two.T, precision[None, :], drift[None, :], terminal, ex1, ex0, flags)
    return handed(one, zero)


def hand(a, b, c, d, sems):
    copies = [pltpu.make_async_copy(a, c, sems.at[0]), pltpu.make_async_copy(b, d, sems.at[1])]
    for copy in copies:
        copy.start()
    for copy in copies:
        copy.wait()


def handed(one, zero):
    here = pl.BlockSpec(memory_space=pltpu.VMEM)
    out = jax.ShapeDtypeStruct(one.shape, one.dtype)
    return pl.pallas_call(
        hand,
        out_shape=(out, out),
        in_specs=[here, here],
        out_specs=(pl.BlockSpec(memory_space=pltpu.HBM),) * 2,
        scratch_shapes=[pltpu.SemaphoreType.DMA((2,))],
        compiler_params=pltpu.CompilerParams(vmem_limit_bytes=2 * 1024 * 1024),
    )(one, zero)


def solution(mesh):
    both = P(("row", "col"), None)
    return jax.shard_map(
        functools.partial(shards, mesh.shape["row"], mesh.shape["col"]),
        mesh=mesh,
        in_specs=(P("row", None), both, P("col", None), P(), P(), P("col", None), both, both, P()),
        out_specs=(both, both),
        check_vma=False,
    )
```

```python
import functools

import jax
import jax.numpy as jnp
from jax import lax
from jax.experimental import pallas as pl
from jax.experimental.pallas import tpu as pltpu
from jax.sharding import PartitionSpec as P

MESH = pl.DeviceIdType.MESH
TILE = 256
PARTS = 4
RELAY = 1
CUTS = 2
LAST = 2
LIMIT = 60 * 1024 * 1024


def flip(index, mask, size):
    bit = 1
    while bit < size:
        if mask & bit:
            index = index + bit - 2 * bit * lax.rem(lax.div(index, bit), 2)
        bit *= 2
    return index


def column_of(row):
    return jnp.broadcast_to(row, (128, row.shape[1])).T[:, :1]


def queries_of(nodes, precision, drift, height):
    shifted = nodes + drift
    offsets = 0.5 * jnp.sum(precision * shifted * shifted, axis=0, keepdims=True)
    first = offsets.astype(jnp.bfloat16).astype(jnp.float32)
    rest = offsets - first
    second = rest.astype(jnp.bfloat16).astype(jnp.float32)
    third = rest - second
    count = height - nodes.shape[0]
    at = lax.broadcasted_iota(jnp.int32, (count, nodes.shape[1]), 0)
    extra = jnp.where(at == 0, first, jnp.where(at == 1, second, jnp.where(at == 2, third, 0.0)))
    return jnp.concatenate([shifted * precision, extra], axis=0)


def upright(tall, lanes):
    short = lanes - tall.shape[0]
    if short:
        tall = jnp.concatenate([tall, jnp.zeros((short, tall.shape[1]), tall.dtype)], axis=0)
    return tall.T.astype(jnp.bfloat16)


def ones_under(count, width):
    at = lax.broadcasted_iota(jnp.int32, (count, width), 0)
    return jnp.where(at < 3, -1.0, 0.0).astype(jnp.bfloat16)


def turned(x):
    mid = x.shape[1] // 2
    return jnp.concatenate([x[:, mid:], x[:, :mid]], axis=1)


def mixed(a, b):
    low = lax.broadcasted_iota(jnp.int32, a.shape, 1) < a.shape[1] // 2
    return jnp.where(low, a, b)


def packed(x):
    top, bottom = x[: x.shape[0] // 2], turned(x[x.shape[0] // 2 :])
    return jnp.concatenate([mixed(top, bottom), mixed(bottom, top)], axis=0)


def unpacked(x):
    a, b = x[: x.shape[0] // 2], x[x.shape[0] // 2 :]
    return jnp.concatenate([mixed(a, b), turned(mixed(b, a))], axis=0)


def floor_of(allowed, exercise):
    return packed(jnp.where(allowed == 1, exercise, -jnp.inf))


def scored(queries, targets):
    s = lax.dot_general(queries, targets, (((1,), (0,)), ((), ())), preferred_element_type=jnp.float32)
    fold = (s.shape[0] // 8, 8, s.shape[1])
    peak = jnp.max(jnp.max(s.reshape(fold), axis=0), axis=0, keepdims=True)
    x = jnp.exp(s - peak)
    return x, peak, jnp.sum(jnp.sum(x.reshape(fold), axis=0), axis=0, keepdims=True)


def merged(levels, totals):
    top = functools.reduce(jnp.maximum, levels)
    total = None
    for i, level in enumerate(levels):
        term = jnp.exp(level - top)
        if totals is not None:
            term = totals[i] * term
        total = term if total is None else total + term
    return top + jnp.log(total)


def body(
    rows,
    cols,
    nz_hbm,
    n1_hbm,
    n2_hbm,
    precision_hbm,
    drift_hbm,
    terminal_hbm,
    ex1_hbm,
    ex0_hbm,
    flags_hbm,
    v1_out,
    v0_out,
    precision_ref,
    drift_ref,
    flags_ref,
    nz_ref,
    n1_ref,
    n2_ref,
    terminal_ref,
    ex1_ref,
    ex0_ref,
    v1_ref,
    v0_ref,
    q1t,
    q1,
    t1,
    q0a,
    q0,
    wz,
    t2,
    e1,
    e0,
    pk1,
    tt1,
    f1,
    pk0,
    tt0,
    f0,
    l1,
    l0p,
    l0,
    price,
    acc1,
    acc0,
    pair_out1,
    pair_in1,
    far_out1,
    far_in1,
    far_out0,
    far_in0,
    q_send,
    q_recv,
    t_send,
    t_recv,
    l1_send,
    l1_recv,
    l0p_send,
    l0p_recv,
    l0_send,
    l0_recv,
    p_send,
    p_recv,
    pc_recv,
    pair1_send,
    pair1_recv,
    far1_send,
    far1_recv,
    y_send,
    y_recv,
    far0_send,
    far0_recv,
    local,
    ready,
):
    r = lax.axis_index("row")
    c = lax.axis_index("col")
    depth, own = n1_ref.shape
    lanes = q0a.shape[1]
    height = q1t.shape[1]
    _, chunks, _, width = e1.shape
    trades = price.shape[2]
    sources = q0a.shape[0]
    blocks, _, _ = pk0.shape
    step = sources // blocks
    half_own = own // 2
    near = sources // 2
    quarter = sources // 4
    group = 2 * lax.div(r, 2) + lax.rem(c, 2)

    def row_peer(m):
        return (flip(r, m, rows), c)

    def col_peer(s):
        return (r, flip(c, s, cols))

    def plane_peer(s):
        return (flip(r, s % 2, rows), flip(c, s - s % 2, cols))

    def remote(src, dst, send, recv, peer):
        return pltpu.make_async_remote_copy(
            src_ref=src, dst_ref=dst, send_sem=send, recv_sem=recv, device_id=peer, device_id_type=MESH
        )

    line = rows // 2
    deep = lax.div(r, 2)
    core = lax.rem(c, 2)
    beside = cols + jnp.where(deep > 0, 1, 0) + jnp.where(deep < line - 1, 1, 0)
    barrier = pltpu.get_barrier_semaphore()

    def call(sem):
        for s in range(1, cols):
            pl.semaphore_signal(sem, inc=1, device_id=col_peer(s), device_id_type=MESH)
        pl.semaphore_signal(sem, inc=1, device_id=row_peer(1), device_id_type=MESH)

        @pl.when(deep > 0)
        def _():
            pl.semaphore_signal(sem, inc=1, device_id=(r - 2, c), device_id_type=MESH)

        @pl.when(deep < line - 1)
        def _():
            pl.semaphore_signal(sem, inc=1, device_id=(r + 2, c), device_id_type=MESH)

    call(barrier)
    loads = [
        pltpu.make_async_copy(a, b, local.at[i])
        for i, (a, b) in enumerate(
            [
                (n1_hbm, n1_ref),
                (precision_hbm, precision_ref),
                (drift_hbm, drift_ref),
                (n2_hbm, n2_ref),
                (nz_hbm, nz_ref),
                (terminal_hbm, terminal_ref),
                (ex1_hbm, ex1_ref),
                (flags_hbm, flags_ref),
                (ex0_hbm, ex0_ref),
            ]
        )
    ]
    for load in loads:
        load.start()
    for load in loads[:3]:
        load.wait()
    precision = column_of(precision_ref[...])
    drift = column_of(drift_ref[...])
    mine = queries_of(n1_ref[...], precision, drift, height)
    q1t[0] = mine.astype(jnp.bfloat16)
    t1[0, :depth, :] = n1_ref[...].astype(jnp.bfloat16)
    pl.semaphore_wait(barrier, beside)
    call(ready.at[0])

    def q_copy(s, peer):
        return remote(q1t.at[0], q1t.at[s], q_send.at[0], q_recv.at[s - 1], peer)

    q_copy(1, col_peer(1)).start()
    for other in range(2):
        for s in range(2, cols, 2):
            slot = s + (1 - core if other else core)
            q_copy(slot, (r, flip(c, s, cols) - core + other)).start()

    def t_copy(m):
        if m % 2:
            src, peer = t1.at[m - 1, pl.ds(0, depth)], col_peer(1)
        else:
            src, peer = t1.at[0, pl.ds(0, depth)], row_peer(m)
        return remote(src, t1.at[m, pl.ds(0, depth)], t_send.at[0], t_recv.at[m % 2 + (2 if m >= 6 else 0)], peer)

    t_copy(1).start()
    if rows > 2:
        t_copy(2).start()

    q1[0] = upright(mine, lanes)
    for m in range(rows):
        t1[m, depth:, :] = ones_under(lanes - depth, own)
    loads[3].wait()
    for k in range(chunks):
        t2[k, :depth, :] = n2_ref[:, k * width : (k + 1) * width].astype(jnp.bfloat16)
        t2[k, depth:, :] = ones_under(lanes - depth, width)

    def stats_one(s):
        for k in range(chunks):
            x, peak, total = scored(q1[s], t2[k])
            e1[s, k] = x
            pk1[s, pl.ds(k, 1), :] = peak
            tt1[s, pl.ds(k, 1), :] = total

    every = (0, 1, 2, 3)

    def stats_zero(m, which):
        row = flip(group, m, rows)
        for b in which:
            x, peak, total = scored(q0[b // 2, b % 2], t1[m])
            e0[m, b * step : (b + 1) * step, :] = x
            pk0[b, pl.ds(row, 1), :] = peak
            tt0[b, pl.ds(row, 1), :] = total

    def take_q(s):
        q_copy(s, col_peer(1)).wait_recv()
        q1[s] = upright(q1t[s].astype(jnp.float32), lanes)

    stats_one(0)
    loads[4].wait()
    q0a[...] = upright(queries_of(nz_ref[...], precision, drift, height), lanes)
    for s in range(0, cols, 2):
        at = pl.multiple_of(flip(c, s, cols) * own, own)
        for side in range(2):
            q0[side, 0, s // 2 * half_own : (s // 2 + 1) * half_own, :] = q0a[pl.ds(at + side * half_own, half_own), :]
    y_copy = remote(q0.at[:, 0], q0.at[:, 1], y_send.at[0], y_recv.at[0], row_peer(1))
    y_copy.start()
    rounds = ready.shape[0]

    def hear(i):
        pl.semaphore_wait(ready.at[i], beside)
        if i + 1 < rounds:
            call(ready.at[i + 1])

    take_q(1)
    hear(0)
    if rows > 4:
        t_copy(4).start()
    stats_one(1)
    stats_zero(0, (0, 2))
    for other in range(2):
        for s in range(2, cols, 2):
            slot = s + (core if other else 1 - core)
            take_q(slot)
            if other == 0 and s == 2:
                for i in range(1, rounds - 1):
                    hear(i)
                for m in range(6, rows, 2):
                    t_copy(m).start()
            stats_one(slot)

    def l1_copy(m):
        return remote(l1.at[0], l1.at[m], l1_send.at[0], l1_recv.at[0], row_peer(m))

    if rounds > 1:
        hear(rounds - 1)
    l1[0] = merged([pk1[s] for s in range(cols)], [tt1[s] for s in range(cols)])
    for m in reversed(range(1, rows)):
        l1_copy(m).start()

    def t_all(count, at):
        view = t1.at[pl.ds(0, count), pl.ds(0, depth)]
        return remote(view, view, t_send.at[0], t_recv.at[at], col_peer(1))

    first_ones, late_ones = range(2, min(6, rows), 2), range(6, rows, 2)
    if first_ones:
        t_all(len(first_ones), 0).wait_recv()
        for m in first_ones:
            t_copy(m + 1).start()
    y_copy.wait_recv()
    stats_zero(0, (1, 3))
    for m in first_ones:
        stats_zero(m, every)
    t_all(1 + len(first_ones), 1).wait_recv()
    if late_ones:
        t_all(len(late_ones), 2).wait_recv()
        for m in late_ones:
            t_copy(m + 1).start()
    for m in [1] + [m + 1 for m in first_ones]:
        stats_zero(m, every)

    def weights_one(s, k):
        return (e1[s, k] * f1[s, k : k + 1, :]).astype(jnp.bfloat16)

    def partial_one(s):
        total = None
        for k in range(chunks):
            part = jnp.dot(
                weights_one(s, k), terminal_ref[k * width : (k + 1) * width, :], preferred_element_type=jnp.float32
            )
            total = part if total is None else total + part
        return packed(total)

    cut = own // CUTS

    def pair_copy(s, h):
        piece = pl.ds(h * cut, cut)
        at = h * (cols // 2) + s // 2
        return remote(
            pair_out1.at[s // 2, piece], pair_in1.at[s // 2, piece], pair1_send.at[0], pair1_recv.at[at], col_peer(1)
        )

    def far_copy(s, h):
        at = h * (cols // 2 - 1) + s // 2 - 1
        piece = pl.ds(h * size, size)
        return remote(
            far_out1.at[s // 2, piece], far_in1.at[s // 2, piece], far1_send.at[0], far1_recv.at[at], col_peer(s)
        )

    def last_copy(s, h):
        piece = pl.ds(h * count, count)
        return remote(far_out0.at[s, piece], far_in0.at[s, piece], far0_send.at[0], far0_recv.at[h], plane_peer(s))

    size = own // PARTS
    count = own // LAST
    away = list(range(2, cols, 2))

    l1_all = remote(l1.at[pl.ds(1, rows - 1)], l1.at[pl.ds(1, rows - 1)], l1_send.at[0], l1_recv.at[0], row_peer(1))
    l1_all.wait_recv()
    loads[5].wait()
    level = merged([l1[m] for m in range(rows)], None)
    for s in range(cols):
        f1[s] = jnp.exp(pk1[s] - level)

    def give(s):
        total = partial_one(s + 1)
        for h in range(CUTS):
            pair_out1[s // 2, h * cut : (h + 1) * cut, :] = total[h * cut : (h + 1) * cut]
            pair_copy(s, h).start()

    for s in away:
        give(s)
    for s in away:
        acc1[s // 2] = partial_one(s)
    give(0)
    for h in range(CUTS):
        for s in away:
            pair_copy(s, h).wait_recv()
            for i in range(h * PARTS // CUTS, (h + 1) * PARTS // CUTS):
                piece = slice(i * size, (i + 1) * size)
                far_out1[s // 2, piece, :] = acc1[s // 2, piece, :] + pair_in1[s // 2, piece, :]
                far_copy(s, i).start()
    for m in late_ones:
        stats_zero(m, every)
    if late_ones:
        t_all(len(late_ones), 3).wait_recv()
    for m in late_ones:
        stats_zero(m + 1, every)
    l0p[0] = merged([pk0[b] for b in range(blocks)], [tt0[b] for b in range(blocks)])
    l0_pair = remote(l0p.at[0], l0p.at[1], l0p_send.at[0], l0p_recv.at[0], col_peer(1))
    l0_pair.start()
    acc1[0] = partial_one(0)
    for load in loads[6:]:
        load.wait()
    ex1_ref[...] = floor_of(flags_ref[1:2, :], ex1_ref[...])
    ex0_ref[...] = floor_of(flags_ref[0:1, :], ex0_ref[...])
    for h in range(CUTS):
        pair_copy(0, h).wait_recv()
    held = acc1[0] + pair_in1[0]
    l0_pair.wait_recv()
    l0[0] = merged([l0p[0], l0p[1]], None)

    def l0_copy(m):
        return remote(l0.at[0], l0.at[m // 2], l0_send.at[0], l0_recv.at[0], row_peer(m))

    for m in reversed(range(2, rows, 2)):
        l0_copy(m).start()

    def p_copy(m, h):
        piece = pl.ds(h * size, size)
        if m % 2:
            src, peer, recv = price.at[m - 1, piece], col_peer(1), pc_recv.at[h * 2 // PARTS * line + m // 2]
        else:
            recv = p_recv.at[h * (rows // 2 - 1) + m // 2 - 1]
            src, peer = (price.at[m - 2, piece], row_peer(2)) if relayed(m, h) else (price.at[0, piece], row_peer(m))
        return remote(src, price.at[m, piece], p_send.at[0], recv, peer)

    def relayed(m, h):
        return h < RELAY and m % 4 == 2 and m > 2

    def p_core(m, half):
        view = price.at[m, pl.ds(half * half_own, half_own)]
        return remote(view, view, p_send.at[0], pc_recv.at[half * line + m // 2], col_peer(1))

    for h in range(PARTS):
        piece = slice(h * size, (h + 1) * size)
        carried = held[piece]
        for s in away:
            far_copy(s, h).wait_recv()
            carried = carried + far_in1[s // 2, piece, :]
        value = jnp.maximum(ex1_ref[piece, :], carried)
        price[0, piece, :] = value.astype(jnp.bfloat16)
        for m in range(rows - 2, 0, -2):
            if not relayed(m, h):
                p_copy(m, h).start()
        p_copy(1, h).start()
        v1_ref[piece, :] = value
    def weigh(m):
        row = flip(group, m, rows)
        for b in range(blocks):
            part = e0[m, b * step : (b + 1) * step, :] * f0[b, pl.ds(row, 1), :]
            wz[m, b * step : (b + 1) * step, :] = part.astype(jnp.bfloat16)

    def sides(m, half):
        p = price[m, half * half_own : (half + 1) * half_own, :].astype(jnp.float32)
        t = turned(p)
        return p, t

    def stacked(a, b):
        return jnp.concatenate([a, b], axis=0).astype(jnp.bfloat16)

    def times(m, first, many, right):
        return jnp.dot(wz[m, pl.ds(first, many), :], right, preferred_element_type=jnp.float32)

    def rights(m, half):
        p = price[m, half * half_own : (half + 1) * half_own, :]
        t = turned(p)
        return m, jnp.concatenate([p, t], axis=0), jnp.concatenate([t, p], axis=0)

    def products(pairs, at):
        upper = lower = None
        for m, right, left in pairs:
            a = times(m, at, quarter, right)
            b = times(m, near + at, quarter, left)
            upper = a if upper is None else upper + a
            lower = b if lower is None else lower + b
        return upper, lower

    def gain_both(slots):
        pairs = []
        for m in slots:
            weigh(m)
            (pa, ta), (pb, tb) = sides(m, 0), sides(m, 1)
            pairs.append((m, stacked(mixed(pa, pb), mixed(ta, tb)), stacked(mixed(tb, ta), mixed(pb, pa))))
        for at in range(0, near, quarter):
            upper, lower = products(pairs, at)
            acc0[0, at : at + quarter, :] = mixed(upper, lower)
            acc0[1, at : at + quarter, :] = mixed(lower, upper)

    def product(pairs, half, at):
        upper, lower = products(pairs, at)
        return mixed(lower, upper) if half else mixed(upper, lower)

    def gain(slots, half):
        pairs = [rights(m, half) for m in slots]
        for at in range(0, near, quarter):
            acc0[half, at : at + quarter, :] = acc0[half, at : at + quarter, :] + product(pairs, half, at)

    def pass_on(m, h):
        p_copy(m, h).wait_recv()
        if m + 2 < rows and relayed(m + 2, h) and m % 4 == 0:
            p_copy(m + 2, h).start()
        p_copy(m + 1, h).start()

    def l0_all():
        view = l0.at[pl.ds(1, rows // 2 - 1)]
        return remote(view, view, l0_send.at[0], l0_recv.at[0], row_peer(1))

    def ready_zero():
        if rows > 2:
            l0_all().wait_recv()
        level = merged([l0[i] for i in range(rows // 2)], None)
        for b in range(blocks):
            f0[b] = jnp.exp(pk0[b] - level)

    direct = [m for m in range(2, rows, 2) if m % 4 == 0 or m == 2]
    other = [m for m in range(2, rows, 2) if m not in direct]
    ahead = [m for m in range(3, rows - 2, 2)]

    def pass_all(h):
        for m in reversed(direct):
            pass_on(m, h)
        for m in other:
            if not relayed(m, h):
                pass_on(m, h)

    def finish(half, slots):
        pairs = [rights(m, half) for m in slots]
        here = slice(half * half_own, (half + 1) * half_own)
        for dy in (1, 0):
            total = acc0[half, dy * quarter : (dy + 1) * quarter, :] + product(pairs, half, dy * quarter)
            for s in [s + dy for s in away] + [dy]:
                part = total[s // 2 * half_own : (s // 2 + 1) * half_own]
                if s:
                    far_out0[s, here, :] = part.astype(far_out0.dtype)
                    last_copy(s, half).start()
                else:
                    v0_ref[here, :] = part

    def take_core(slots, half):
        for m in slots:
            p_core(m, half).wait_recv()

    ends = other + ([rows - 1] if rows > 2 else [])
    pass_all(0)
    ready_zero()
    for half in range(2):
        p_core(1, half).wait_recv()
    gain_both([0, 1])
    for m in range(2, rows):
        weigh(m)
    v1_ref[...] = unpacked(v1_ref[...])
    keep_one = pltpu.make_async_copy(v1_ref, v1_out, local.at[9])
    keep_one.start()
    for h in range(1, PARTS // 2):
        pass_all(h)
    gain(direct, 0)
    for h in range(min(RELAY, PARTS // 2)):
        for m in other:
            pass_on(m, h)
    pass_all(PARTS // 2)
    take_core(ahead, 0)
    for h in range(PARTS // 2 + 1, PARTS):
        pass_all(h)
    if ahead:
        gain(ahead, 0)
    take_core([rows - 1], 0)
    finish(0, ends)
    gain(direct, 1)
    take_core(ahead + [rows - 1], 1)
    finish(1, ahead + ends)
    for h in range(LAST):
        piece = slice(h * count, (h + 1) * count)
        view = far_in0.at[pl.ds(1, cols - 1), pl.ds(h * count, count)]
        remote(view, view, far0_send.at[0], far0_recv.at[h], col_peer(1)).wait_recv()
        carried = v0_ref[piece, :]
        for s in range(1, cols):
            carried = carried + far_in0[s, piece, :].astype(jnp.float32)
        v0_ref[piece, :] = jnp.maximum(ex0_ref[piece, :], carried)
    v0_ref[...] = unpacked(v0_ref[...])
    keep_zero = pltpu.make_async_copy(v0_ref, v0_out, local.at[10])
    keep_zero.start()

    y_copy.wait_send()

    def sent(ref, first, count, sem):
        view = ref.at[pl.ds(first, count)]
        remote(view, view, sem.at[0], y_recv.at[0], col_peer(1)).wait_send()

    sent(q1t, 0, cols - 1, q_send)
    t_all(rows - 1, 0).wait_send()
    l1_all.wait_send()
    l0_pair.wait_send()
    if rows > 2:
        l0_all().wait_send()
    sent(price, 0, rows - 1, p_send)
    sent(pair_out1, 0, cols // 2, pair1_send)
    if away:
        sent(far_out1, 1, cols // 2 - 1, far1_send)
    sent(far_out0, 1, cols - 1, far0_send)
    keep_one.wait()
    keep_zero.wait()


def shards(rows, cols, nodes_zero, nodes_one, nodes_two, precision, drift, terminal, ex1, ex0, flags):
    own, depth = nodes_one.shape
    height = depth + 16
    sources = nodes_zero.shape[0]
    targets = nodes_two.shape[0]
    trades = terminal.shape[1]
    width = min(TILE, targets)
    chunks = targets // width
    blocks = 4
    lanes = 128 * (-(-(depth + 3) // 128))
    dma = pltpu.SemaphoreType.DMA
    f32, bf16 = jnp.float32, jnp.bfloat16
    row_stat = pltpu.VMEM((cols, chunks, width), f32)
    col_stat = pltpu.VMEM((blocks, rows, own), f32)
    piece = pltpu.VMEM((cols // 2, own, trades), f32)
    slim = pltpu.VMEM((cols, own, trades), bf16)
    mine = pltpu.VMEM((own, trades), f32)
    one, zero = pl.pallas_call(
        functools.partial(body, rows, cols),
        out_shape=(pltpu.VMEM((own, trades), f32),) * 2,
        in_specs=[pl.BlockSpec(memory_space=pltpu.HBM)] * 9,
        out_specs=(pl.BlockSpec(memory_space=pl.ANY),) * 2,
        scratch_shapes=[
            pltpu.VMEM((1, depth), f32),
            pltpu.VMEM((1, depth), f32),
            pltpu.VMEM((2, trades), jnp.int32),
            pltpu.VMEM((depth, sources), f32),
            pltpu.VMEM((depth, own), f32),
            pltpu.VMEM((depth, targets), f32),
            pltpu.VMEM((targets, trades), bf16),
            *[mine] * 4,
            pltpu.VMEM((cols, height, own), bf16),
            pltpu.VMEM((cols, own, lanes), bf16),
            pltpu.VMEM((rows, lanes, own), bf16),
            pltpu.VMEM((sources, lanes), bf16),
            pltpu.VMEM((2, 2, sources // 4, lanes), bf16),
            pltpu.VMEM((rows, sources, own), bf16),
            pltpu.VMEM((chunks, lanes, width), bf16),
            pltpu.VMEM((cols, chunks, own, width), f32),
            pltpu.VMEM((rows, sources, own), f32),
            row_stat,
            row_stat,
            row_stat,
            col_stat,
            col_stat,
            col_stat,
            pltpu.VMEM((rows, chunks, width), f32),
            pltpu.VMEM((2, rows, own), f32),
            pltpu.VMEM((rows // 2, rows, own), f32),
            pltpu.VMEM((rows, own, trades), bf16),
            piece,
            pltpu.VMEM((2, sources // 2, trades), f32),
            *[piece] * 4,
            *[slim] * 2,
            dma((1,)),
            dma((cols - 1,)),
            dma((1,)),
            dma((4,)),
            *[dma((1,))] * 7,
            dma((PARTS * max(1, rows // 2 - 1),)),
            dma((rows,)),
            dma((1,)),
            dma((CUTS * (cols // 2),)),
            dma((1,)),
            dma((PARTS * max(1, cols // 2 - 1),)),
            *[dma((1,))] * 3,
            dma((LAST,)),
            dma((11,)),
            pltpu.SemaphoreType.REGULAR((max(1, rows // 2 - 1),)),
        ],
        compiler_params=pltpu.CompilerParams(
            collective_id=0, has_side_effects=True, vmem_limit_bytes=LIMIT
        ),
    )(nodes_zero.T, nodes_one.T, nodes_two.T, precision[None, :], drift[None, :], terminal, ex1, ex0, flags)
    return handed(one, zero)


def hand(a, b, c, d, sems):
    copies = [pltpu.make_async_copy(a, c, sems.at[0]), pltpu.make_async_copy(b, d, sems.at[1])]
    for copy in copies:
        copy.start()
    for copy in copies:
        copy.wait()


def handed(one, zero):
    here = pl.BlockSpec(memory_space=pltpu.VMEM)
    out = jax.ShapeDtypeStruct(one.shape, one.dtype)
    return pl.pallas_call(
        hand,
        out_shape=(out, out),
        in_specs=[here, here],
        out_specs=(pl.BlockSpec(memory_space=pltpu.HBM),) * 2,
        scratch_shapes=[pltpu.SemaphoreType.DMA((2,))],
        compiler_params=pltpu.CompilerParams(vmem_limit_bytes=2 * 1024 * 1024),
    )(one, zero)


def solution(mesh):
    both = P(("row", "col"), None)
    return jax.shard_map(
        functools.partial(shards, mesh.shape["row"], mesh.shape["col"]),
        mesh=mesh,
        in_specs=(P("row", None), both, P("col", None), P(), P(), P("col", None), both, both, P()),
        out_specs=(both, both),
        check_vma=False,
    )
```

```python
import functools

import jax
import jax.numpy as jnp
from jax import lax
from jax.experimental import pallas as pl
from jax.experimental.pallas import tpu as pltpu
from jax.sharding import PartitionSpec as P

MESH = pl.DeviceIdType.MESH
TILE = 256
PARTS = 4
RELAY = 1
CUTS = 2
LAST = 2
LIMIT = 60 * 1024 * 1024


def flip(index, mask, size):
    bit = 1
    while bit < size:
        if mask & bit:
            index = index + bit - 2 * bit * lax.rem(lax.div(index, bit), 2)
        bit *= 2
    return index


def column_of(row):
    return jnp.broadcast_to(row, (128, row.shape[1])).T[:, :1]


def queries_of(nodes, precision, drift, height):
    shifted = nodes + drift
    offsets = 0.5 * jnp.sum(precision * shifted * shifted, axis=0, keepdims=True)
    first = offsets.astype(jnp.bfloat16).astype(jnp.float32)
    rest = offsets - first
    second = rest.astype(jnp.bfloat16).astype(jnp.float32)
    third = rest - second
    count = height - nodes.shape[0]
    at = lax.broadcasted_iota(jnp.int32, (count, nodes.shape[1]), 0)
    extra = jnp.where(at == 0, first, jnp.where(at == 1, second, jnp.where(at == 2, third, 0.0)))
    return jnp.concatenate([shifted * precision, extra], axis=0)


def upright(tall, lanes):
    short = lanes - tall.shape[0]
    if short:
        tall = jnp.concatenate([tall, jnp.zeros((short, tall.shape[1]), tall.dtype)], axis=0)
    return tall.T.astype(jnp.bfloat16)


def ones_under(count, width):
    at = lax.broadcasted_iota(jnp.int32, (count, width), 0)
    return jnp.where(at < 3, -1.0, 0.0).astype(jnp.bfloat16)


def turned(x):
    mid = x.shape[1] // 2
    return jnp.concatenate([x[:, mid:], x[:, :mid]], axis=1)


def mixed(a, b):
    low = lax.broadcasted_iota(jnp.int32, a.shape, 1) < a.shape[1] // 2
    return jnp.where(low, a, b)


def packed(x):
    top, bottom = x[: x.shape[0] // 2], turned(x[x.shape[0] // 2 :])
    return jnp.concatenate([mixed(top, bottom), mixed(bottom, top)], axis=0)


def unpacked(x):
    a, b = x[: x.shape[0] // 2], x[x.shape[0] // 2 :]
    return jnp.concatenate([mixed(a, b), turned(mixed(b, a))], axis=0)


def floor_of(allowed, exercise):
    return packed(jnp.where(allowed == 1, exercise, -jnp.inf))


def scored(queries, targets):
    s = lax.dot_general(queries, targets, (((1,), (0,)), ((), ())), preferred_element_type=jnp.float32)
    fold = (s.shape[0] // 8, 8, s.shape[1])
    peak = jnp.max(jnp.max(s.reshape(fold), axis=0), axis=0, keepdims=True)
    x = jnp.exp(s - peak)
    return x, peak, jnp.sum(jnp.sum(x.reshape(fold), axis=0), axis=0, keepdims=True)


def merged(levels, totals):
    top = functools.reduce(jnp.maximum, levels)
    total = None
    for i, level in enumerate(levels):
        term = jnp.exp(level - top)
        if totals is not None:
            term = totals[i] * term
        total = term if total is None else total + term
    return top + jnp.log(total)


def body(
    rows,
    cols,
    nz_hbm,
    n1_hbm,
    n2_hbm,
    precision_hbm,
    drift_hbm,
    terminal_hbm,
    ex1_hbm,
    ex0_hbm,
    flags_hbm,
    v1_out,
    v0_out,
    precision_ref,
    drift_ref,
    flags_ref,
    nz_ref,
    n1_ref,
    n2_ref,
    terminal_ref,
    ex1_ref,
    ex0_ref,
    v1_ref,
    v0_ref,
    q1t,
    q1,
    t1,
    q0a,
    q0,
    wz,
    t2,
    e1,
    e0,
    pk1,
    tt1,
    f1,
    pk0,
    tt0,
    f0,
    l1,
    l0p,
    l0,
    price,
    acc1,
    acc0,
    pair_out1,
    pair_in1,
    far_out1,
    far_in1,
    far_out0,
    far_in0,
    q_send,
    q_recv,
    t_send,
    t_recv,
    l1_send,
    l1_recv,
    l0p_send,
    l0p_recv,
    l0_send,
    l0_recv,
    p_send,
    p_recv,
    pc_recv,
    pair1_send,
    pair1_recv,
    far1_send,
    far1_recv,
    y_send,
    y_recv,
    far0_send,
    far0_recv,
    local,
    ready,
):
    r = lax.axis_index("row")
    c = lax.axis_index("col")
    depth, own = n1_ref.shape
    lanes = q0a.shape[1]
    height = q1t.shape[1]
    _, chunks, _, width = e1.shape
    trades = price.shape[2]
    sources = q0a.shape[0]
    blocks, _, _ = pk0.shape
    step = sources // blocks
    half_own = own // 2
    near = sources // 2
    quarter = sources // 4
    group = 2 * lax.div(r, 2) + lax.rem(c, 2)

    def row_peer(m):
        return (flip(r, m, rows), c)

    def col_peer(s):
        return (r, flip(c, s, cols))

    def plane_peer(s):
        return (flip(r, s % 2, rows), flip(c, s - s % 2, cols))

    def remote(src, dst, send, recv, peer):
        return pltpu.make_async_remote_copy(
            src_ref=src, dst_ref=dst, send_sem=send, recv_sem=recv, device_id=peer, device_id_type=MESH
        )

    line = rows // 2
    deep = lax.div(r, 2)
    core = lax.rem(c, 2)
    beside = cols + jnp.where(deep > 0, 1, 0) + jnp.where(deep < line - 1, 1, 0)
    barrier = pltpu.get_barrier_semaphore()

    def call(sem):
        for s in range(1, cols):
            pl.semaphore_signal(sem, inc=1, device_id=col_peer(s), device_id_type=MESH)
        pl.semaphore_signal(sem, inc=1, device_id=row_peer(1), device_id_type=MESH)

        @pl.when(deep > 0)
        def _():
            pl.semaphore_signal(sem, inc=1, device_id=(r - 2, c), device_id_type=MESH)

        @pl.when(deep < line - 1)
        def _():
            pl.semaphore_signal(sem, inc=1, device_id=(r + 2, c), device_id_type=MESH)

    call(barrier)
    loads = [
        pltpu.make_async_copy(a, b, local.at[i])
        for i, (a, b) in enumerate(
            [
                (n1_hbm, n1_ref),
                (precision_hbm, precision_ref),
                (drift_hbm, drift_ref),
                (n2_hbm, n2_ref),
                (nz_hbm, nz_ref),
                (terminal_hbm, terminal_ref),
                (ex1_hbm, ex1_ref),
                (flags_hbm, flags_ref),
                (ex0_hbm, ex0_ref),
            ]
        )
    ]
    for load in loads:
        load.start()
    for load in loads[:3]:
        load.wait()
    precision = column_of(precision_ref[...])
    drift = column_of(drift_ref[...])
    mine = queries_of(n1_ref[...], precision, drift, height)
    q1t[0] = mine.astype(jnp.bfloat16)
    t1[0, :depth, :] = n1_ref[...].astype(jnp.bfloat16)
    pl.semaphore_wait(barrier, beside)
    call(ready.at[0])

    def q_copy(s, peer):
        return remote(q1t.at[0], q1t.at[s], q_send.at[0], q_recv.at[s - 1], peer)

    q_copy(1, col_peer(1)).start()
    for other in range(2):
        for s in range(2, cols, 2):
            slot = s + (1 - core if other else core)
            q_copy(slot, (r, flip(c, s, cols) - core + other)).start()

    def t_copy(m):
        if m % 2:
            src, peer = t1.at[m - 1, pl.ds(0, depth)], col_peer(1)
        else:
            src, peer = t1.at[0, pl.ds(0, depth)], row_peer(m)
        return remote(src, t1.at[m, pl.ds(0, depth)], t_send.at[0], t_recv.at[m % 2 + (2 if m >= 6 else 0)], peer)

    t_copy(1).start()
    if rows > 2:
        t_copy(2).start()

    q1[0] = upright(mine, lanes)
    for m in range(rows):
        t1[m, depth:, :] = ones_under(lanes - depth, own)
    loads[3].wait()
    for k in range(chunks):
        t2[k, :depth, :] = n2_ref[:, k * width : (k + 1) * width].astype(jnp.bfloat16)
        t2[k, depth:, :] = ones_under(lanes - depth, width)

    def stats_one(s):
        for k in range(chunks):
            x, peak, total = scored(q1[s], t2[k])
            e1[s, k] = x
            pk1[s, pl.ds(k, 1), :] = peak
            tt1[s, pl.ds(k, 1), :] = total

    every = (0, 1, 2, 3)

    def stats_zero(m, which):
        row = flip(group, m, rows)
        for b in which:
            x, peak, total = scored(q0[b // 2, b % 2], t1[m])
            e0[m, b * step : (b + 1) * step, :] = x
            pk0[b, pl.ds(row, 1), :] = peak
            tt0[b, pl.ds(row, 1), :] = total

    def take_q(s):
        q_copy(s, col_peer(1)).wait_recv()
        q1[s] = upright(q1t[s], lanes)

    stats_one(0)
    loads[4].wait()
    q0a[...] = upright(queries_of(nz_ref[...], precision, drift, height), lanes)
    for s in range(0, cols, 2):
        at = pl.multiple_of(flip(c, s, cols) * own, own)
        for side in range(2):
            q0[side, 0, s // 2 * half_own : (s // 2 + 1) * half_own, :] = q0a[pl.ds(at + side * half_own, half_own), :]
    y_copy = remote(q0.at[:, 0], q0.at[:, 1], y_send.at[0], y_recv.at[0], row_peer(1))
    y_copy.start()
    rounds = ready.shape[0]

    def hear(i):
        pl.semaphore_wait(ready.at[i], beside)
        if i + 1 < rounds:
            call(ready.at[i + 1])

    take_q(1)
    hear(0)
    if rows > 4:
        t_copy(4).start()
    stats_one(1)
    stats_zero(0, (0, 2))
    for other in range(2):
        for s in range(2, cols, 2):
            slot = s + (core if other else 1 - core)
            take_q(slot)
            if other == 0 and s == 2:
                for i in range(1, rounds - 1):
                    hear(i)
                for m in range(6, rows, 2):
                    t_copy(m).start()
            stats_one(slot)

    def l1_copy(m):
        return remote(l1.at[0], l1.at[m], l1_send.at[0], l1_recv.at[0], row_peer(m))

    if rounds > 1:
        hear(rounds - 1)
    l1[0] = merged([pk1[s] for s in range(cols)], [tt1[s] for s in range(cols)])
    for m in reversed(range(1, rows)):
        l1_copy(m).start()

    def t_all(count, at):
        view = t1.at[pl.ds(0, count), pl.ds(0, depth)]
        return remote(view, view, t_send.at[0], t_recv.at[at], col_peer(1))

    first_ones, late_ones = range(2, min(6, rows), 2), range(6, rows, 2)
    if first_ones:
        t_all(len(first_ones), 0).wait_recv()
        for m in first_ones:
            t_copy(m + 1).start()
    y_copy.wait_recv()
    stats_zero(0, (1, 3))
    for m in first_ones:
        stats_zero(m, every)
    t_all(1 + len(first_ones), 1).wait_recv()
    if late_ones:
        t_all(len(late_ones), 2).wait_recv()
        for m in late_ones:
            t_copy(m + 1).start()
    for m in [1] + [m + 1 for m in first_ones]:
        stats_zero(m, every)

    def weights_one(s, k):
        return (e1[s, k] * f1[s, k : k + 1, :]).astype(jnp.bfloat16)

    def partial_one(s):
        total = None
        for k in range(chunks):
            part = jnp.dot(
                weights_one(s, k), terminal_ref[k * width : (k + 1) * width, :], preferred_element_type=jnp.float32
            )
            total = part if total is None else total + part
        return packed(total)

    cut = own // CUTS

    def pair_copy(s, h):
        piece = pl.ds(h * cut, cut)
        at = h * (cols // 2) + s // 2
        return remote(
            pair_out1.at[s // 2, piece], pair_in1.at[s // 2, piece], pair1_send.at[0], pair1_recv.at[at], col_peer(1)
        )

    def far_copy(s, h):
        at = h * (cols // 2 - 1) + s // 2 - 1
        piece = pl.ds(h * size, size)
        return remote(
            far_out1.at[s // 2, piece], far_in1.at[s // 2, piece], far1_send.at[0], far1_recv.at[at], col_peer(s)
        )

    def last_copy(s, h):
        piece = pl.ds(h * count, count)
        return remote(far_out0.at[s, piece], far_in0.at[s, piece], far0_send.at[0], far0_recv.at[h], plane_peer(s))

    size = own // PARTS
    count = own // LAST
    away = list(range(2, cols, 2))

    l1_all = remote(l1.at[pl.ds(1, rows - 1)], l1.at[pl.ds(1, rows - 1)], l1_send.at[0], l1_recv.at[0], row_peer(1))
    l1_all.wait_recv()
    loads[5].wait()
    level = merged([l1[m] for m in range(rows)], None)
    for s in range(cols):
        f1[s] = jnp.exp(pk1[s] - level)

    def give(s):
        total = partial_one(s + 1)
        for h in range(CUTS):
            pair_out1[s // 2, h * cut : (h + 1) * cut, :] = total[h * cut : (h + 1) * cut]
            pair_copy(s, h).start()

    for s in away:
        give(s)
    for s in away:
        acc1[s // 2] = partial_one(s)
    give(0)
    for h in range(CUTS):
        for s in away:
            pair_copy(s, h).wait_recv()
            for i in range(h * PARTS // CUTS, (h + 1) * PARTS // CUTS):
                piece = slice(i * size, (i + 1) * size)
                far_out1[s // 2, piece, :] = acc1[s // 2, piece, :] + pair_in1[s // 2, piece, :]
                far_copy(s, i).start()
    for m in late_ones:
        stats_zero(m, every)
    if late_ones:
        t_all(len(late_ones), 3).wait_recv()
    for m in late_ones:
        stats_zero(m + 1, every)
    l0p[0] = merged([pk0[b] for b in range(blocks)], [tt0[b] for b in range(blocks)])
    l0_pair = remote(l0p.at[0], l0p.at[1], l0p_send.at[0], l0p_recv.at[0], col_peer(1))
    l0_pair.start()
    acc1[0] = partial_one(0)
    for load in loads[6:]:
        load.wait()
    ex1_ref[...] = floor_of(flags_ref[1:2, :], ex1_ref[...])
    ex0_ref[...] = floor_of(flags_ref[0:1, :], ex0_ref[...])
    for h in range(CUTS):
        pair_copy(0, h).wait_recv()
    held = acc1[0] + pair_in1[0]
    l0_pair.wait_recv()
    l0[0] = merged([l0p[0], l0p[1]], None)

    def l0_copy(m):
        return remote(l0.at[0], l0.at[m // 2], l0_send.at[0], l0_recv.at[0], row_peer(m))

    for m in reversed(range(2, rows, 2)):
        l0_copy(m).start()

    def p_copy(m, h):
        piece = pl.ds(h * size, size)
        if m % 2:
            src, peer, recv = price.at[m - 1, piece], col_peer(1), pc_recv.at[h * 2 // PARTS * line + m // 2]
        else:
            recv = p_recv.at[PARTS + h * (rows // 2) + m // 2 if relayed(m, h) else h]
            src, peer = (price.at[m - 2, piece], row_peer(2)) if relayed(m, h) else (price.at[0, piece], row_peer(m))
        return remote(src, price.at[m, piece], p_send.at[0], recv, peer)

    def relayed(m, h):
        return h < RELAY and m % 4 == 2 and m > 2

    def p_core(m, half):
        view = price.at[m, pl.ds(half * half_own, half_own)]
        return remote(view, view, p_send.at[0], pc_recv.at[half * line + m // 2], col_peer(1))

    for h in range(PARTS):
        piece = slice(h * size, (h + 1) * size)
        carried = held[piece]
        for s in away:
            far_copy(s, h).wait_recv()
            carried = carried + far_in1[s // 2, piece, :]
        value = jnp.maximum(ex1_ref[piece, :], carried)
        price[0, piece, :] = value.astype(jnp.bfloat16)
        for m in range(rows - 2, 0, -2):
            if not relayed(m, h):
                p_copy(m, h).start()
        p_copy(1, h).start()
        v1_ref[piece, :] = value
    def weigh(m):
        row = flip(group, m, rows)
        for b in range(blocks):
            part = e0[m, b * step : (b + 1) * step, :] * f0[b, pl.ds(row, 1), :]
            wz[m, b * step : (b + 1) * step, :] = part.astype(jnp.bfloat16)

    def sides(m, half):
        p = price[m, half * half_own : (half + 1) * half_own, :].astype(jnp.float32)
        t = turned(p)
        return p, t

    def stacked(a, b):
        return jnp.concatenate([a, b], axis=0).astype(jnp.bfloat16)

    def times(m, first, many, right):
        return jnp.dot(wz[m, pl.ds(first, many), :], right, preferred_element_type=jnp.float32)

    def rights(m, half):
        p = price[m, half * half_own : (half + 1) * half_own, :]
        t = turned(p)
        return m, jnp.concatenate([p, t], axis=0), jnp.concatenate([t, p], axis=0)

    def products(pairs, at):
        upper = lower = None
        for m, right, left in pairs:
            a = times(m, at, quarter, right)
            b = times(m, near + at, quarter, left)
            upper = a if upper is None else upper + a
            lower = b if lower is None else lower + b
        return upper, lower

    def gain_both(slots):
        pairs = []
        for m in slots:
            weigh(m)
            (pa, ta), (pb, tb) = sides(m, 0), sides(m, 1)
            pairs.append((m, stacked(mixed(pa, pb), mixed(ta, tb)), stacked(mixed(tb, ta), mixed(pb, pa))))
        for at in range(0, near, quarter):
            upper, lower = products(pairs, at)
            acc0[0, at : at + quarter, :] = mixed(upper, lower)
            acc0[1, at : at + quarter, :] = mixed(lower, upper)

    def product(pairs, half, at):
        upper, lower = products(pairs, at)
        return mixed(lower, upper) if half else mixed(upper, lower)

    def gain(slots, half):
        pairs = [rights(m, half) for m in slots]
        for at in range(0, near, quarter):
            acc0[half, at : at + quarter, :] = acc0[half, at : at + quarter, :] + product(pairs, half, at)

    def pass_on(m, h):
        if relayed(m, h):
            p_copy(m, h).wait_recv()
        if m + 2 < rows and relayed(m + 2, h) and m % 4 == 0:
            p_copy(m + 2, h).start()
        p_copy(m + 1, h).start()

    def l0_all():
        view = l0.at[pl.ds(1, rows // 2 - 1)]
        return remote(view, view, l0_send.at[0], l0_recv.at[0], row_peer(1))

    def ready_zero():
        if rows > 2:
            l0_all().wait_recv()
        level = merged([l0[i] for i in range(rows // 2)], None)
        for b in range(blocks):
            f0[b] = jnp.exp(pk0[b] - level)

    direct = [m for m in range(2, rows, 2) if m % 4 == 0 or m == 2]
    other = [m for m in range(2, rows, 2) if m not in direct]
    ahead = [m for m in range(3, rows - 2, 2)]

    def pass_all(h):
        view = price.at[pl.ds(0, sum(not relayed(m, h) for m in range(2, rows, 2))), pl.ds(h * size, size)]
        remote(view, view, p_send.at[0], p_recv.at[h], col_peer(1)).wait_recv()
        for m in reversed(direct):
            pass_on(m, h)
        for m in other:
            if not relayed(m, h):
                pass_on(m, h)

    def finish(half, slots):
        pairs = [rights(m, half) for m in slots]
        here = slice(half * half_own, (half + 1) * half_own)
        for dy in (1, 0):
            total = acc0[half, dy * quarter : (dy + 1) * quarter, :] + product(pairs, half, dy * quarter)
            for s in [s + dy for s in away] + [dy]:
                part = total[s // 2 * half_own : (s // 2 + 1) * half_own]
                if s:
                    far_out0[s, here, :] = part.astype(far_out0.dtype)
                    last_copy(s, half).start()
                else:
                    v0_ref[here, :] = part

    def take_core(slots, half):
        for m in slots:
            p_core(m, half).wait_recv()

    ends = other + ([rows - 1] if rows > 2 else [])
    pass_all(0)
    ready_zero()
    for half in range(2):
        p_core(1, half).wait_recv()
    gain_both([0, 1])
    for m in range(2, rows):
        weigh(m)
    v1_ref[...] = unpacked(v1_ref[...])
    keep_one = pltpu.make_async_copy(v1_ref, v1_out, local.at[0])
    keep_one.start()
    for h in range(1, PARTS // 2):
        pass_all(h)
    gain(direct, 0)
    for h in range(min(RELAY, PARTS // 2)):
        for m in other:
            pass_on(m, h)
    pass_all(PARTS // 2)
    take_core(ahead, 0)
    for h in range(PARTS // 2 + 1, PARTS):
        pass_all(h)
    if ahead:
        gain(ahead, 0)
    take_core([rows - 1], 0)
    finish(0, ends)
    gain(direct, 1)
    take_core(ahead + [rows - 1], 1)
    finish(1, ahead + ends)
    for h in range(LAST):
        piece = slice(h * count, (h + 1) * count)
        view = far_in0.at[pl.ds(1, cols - 1), pl.ds(h * count, count)]
        remote(view, view, far0_send.at[0], far0_recv.at[h], col_peer(1)).wait_recv()
        carried = v0_ref[piece, :]
        for s in range(1, cols):
            carried = carried + far_in0[s, piece, :].astype(jnp.float32)
        v0_ref[piece, :] = jnp.maximum(ex0_ref[piece, :], carried)
    v0_ref[...] = unpacked(v0_ref[...])
    keep_zero = pltpu.make_async_copy(v0_ref, v0_out, local.at[1])
    keep_zero.start()

    y_copy.wait_send()

    def sent(ref, first, count, sem):
        view = ref.at[pl.ds(first, count)]
        remote(view, view, sem.at[0], y_recv.at[0], col_peer(1)).wait_send()

    sent(q1t, 0, cols - 1, q_send)
    t_all(rows - 1, 0).wait_send()
    l1_all.wait_send()
    l0_pair.wait_send()
    if rows > 2:
        l0_all().wait_send()
    sent(price, 0, rows - 1, p_send)
    sent(pair_out1, 0, cols // 2, pair1_send)
    if away:
        sent(far_out1, 1, cols // 2 - 1, far1_send)
    sent(far_out0, 1, cols - 1, far0_send)
    keep_one.wait()
    keep_zero.wait()


def shards(rows, cols, nodes_zero, nodes_one, nodes_two, precision, drift, terminal, ex1, ex0, flags):
    own, depth = nodes_one.shape
    height = depth + 16
    sources = nodes_zero.shape[0]
    targets = nodes_two.shape[0]
    trades = terminal.shape[1]
    width = min(TILE, targets)
    chunks = targets // width
    blocks = 4
    lanes = 128 * (-(-(depth + 3) // 128))
    dma = pltpu.SemaphoreType.DMA
    f32, bf16 = jnp.float32, jnp.bfloat16
    row_stat = pltpu.VMEM((cols, chunks, width), f32)
    col_stat = pltpu.VMEM((blocks, rows, own), f32)
    piece = pltpu.VMEM((cols // 2, own, trades), f32)
    slim = pltpu.VMEM((cols, own, trades), bf16)
    mine = pltpu.VMEM((own, trades), f32)
    one, zero = pl.pallas_call(
        functools.partial(body, rows, cols),
        out_shape=(pltpu.VMEM((own, trades), f32),) * 2,
        in_specs=[pl.BlockSpec(memory_space=pltpu.HBM)] * 9,
        out_specs=(pl.BlockSpec(memory_space=pl.ANY),) * 2,
        scratch_shapes=[
            pltpu.VMEM((1, depth), f32),
            pltpu.VMEM((1, depth), f32),
            pltpu.VMEM((2, trades), jnp.int32),
            pltpu.VMEM((depth, sources), f32),
            pltpu.VMEM((depth, own), f32),
            pltpu.VMEM((depth, targets), f32),
            pltpu.VMEM((targets, trades), bf16),
            *[mine] * 4,
            pltpu.VMEM((cols, height, own), bf16),
            pltpu.VMEM((cols, own, lanes), bf16),
            pltpu.VMEM((rows, lanes, own), bf16),
            pltpu.VMEM((sources, lanes), bf16),
            pltpu.VMEM((2, 2, sources // 4, lanes), bf16),
            pltpu.VMEM((rows, sources, own), bf16),
            pltpu.VMEM((chunks, lanes, width), bf16),
            pltpu.VMEM((cols, chunks, own, width), f32),
            pltpu.VMEM((rows, sources, own), f32),
            row_stat,
            row_stat,
            row_stat,
            col_stat,
            col_stat,
            col_stat,
            pltpu.VMEM((rows, chunks, width), f32),
            pltpu.VMEM((2, rows, own), f32),
            pltpu.VMEM((rows // 2, rows, own), f32),
            pltpu.VMEM((rows, own, trades), bf16),
            piece,
            pltpu.VMEM((2, sources // 2, trades), f32),
            *[piece] * 4,
            *[slim] * 2,
            dma((1,)),
            dma((cols - 1,)),
            dma((1,)),
            dma((4,)),
            *[dma((1,))] * 7,
            dma((PARTS + max(0, RELAY - 1) * (rows // 2) + rows // 2,)),
            dma((rows,)),
            dma((1,)),
            dma((CUTS * (cols // 2),)),
            dma((1,)),
            dma((PARTS * max(1, cols // 2 - 1),)),
            *[dma((1,))] * 3,
            dma((LAST,)),
            dma((9,)),
            pltpu.SemaphoreType.REGULAR((max(1, rows // 2 - 1),)),
        ],
        compiler_params=pltpu.CompilerParams(
            collective_id=0, has_side_effects=True, vmem_limit_bytes=LIMIT
        ),
    )(nodes_zero.T, nodes_one.T, nodes_two.T, precision[None, :], drift[None, :], terminal, ex1, ex0, flags)
    return handed(one, zero)


def hand(a, b, c, d, sems):
    copies = [pltpu.make_async_copy(a, c, sems.at[0]), pltpu.make_async_copy(b, d, sems.at[1])]
    for copy in copies:
        copy.start()
    for copy in copies:
        copy.wait()


def handed(one, zero):
    here = pl.BlockSpec(memory_space=pltpu.VMEM)
    out = jax.ShapeDtypeStruct(one.shape, one.dtype)
    return pl.pallas_call(
        hand,
        out_shape=(out, out),
        in_specs=[here, here],
        out_specs=(pl.BlockSpec(memory_space=pltpu.HBM),) * 2,
        scratch_shapes=[pltpu.SemaphoreType.DMA((2,))],
        compiler_params=pltpu.CompilerParams(vmem_limit_bytes=2 * 1024 * 1024),
    )(one, zero)


def solution(mesh):
    both = P(("row", "col"), None)
    return jax.shard_map(
        functools.partial(shards, mesh.shape["row"], mesh.shape["col"]),
        mesh=mesh,
        in_specs=(P("row", None), both, P("col", None), P(), P(), P("col", None), both, both, P()),
        out_specs=(both, both),
        check_vma=False,
    )
```
